128 devices in a mesh: group: 8 (over z, core), shard: 8 (over y_lo, x), side: 2 (over y_hi).
Axes of the slice: x: 4, y: 4 (y_hi: 2, y_lo: 2; y = y_hi * 2 + y_lo), z: 4, core: 2. Of those that a mesh axis runs over, the one named last changes fastest.
Arguments:
- master: float32 [64, 2048, 768], P('group', ('shard', 'side')), may hold values from -0.125 to 0.125
- momentum: float32 [64, 2048, 768], P('group', ('shard', 'side')), may hold values from -24 to 24
- gradient: bfloat16 [64, 2048, 768], P('group', ('shard', 'side')), may hold values from -6 to 6
- up_weight: bfloat16 [64, 768, 2048], P(('group', 'shard'), 'side'), may hold values from -0.125 to 0.125
- down_weight: bfloat16 [64, 768, 2048], P(('group', 'shard'), 'side'), may hold values from -0.21875 to 0.21875
- tokens: bfloat16 [512, 2048], replicated, may hold values from -6 to 6
- routes: int32 [512, 8], replicated, may hold values from 0 to 63, all different within a row; in each aligned block of 512 rows (0 to 511, 512 to 1023, ...) at most 128 rows name the same one
- route_weight: float32 [512, 8], replicated, may hold values from 0.1 to 1
Outputs:
- new_master: float32 [64, 2048, 768], P('group', ('shard', 'side'))
- new_momentum: float32 [64, 2048, 768], P('group', ('shard', 'side'))
- combined: bfloat16 [512, 2048], P(('group', 'shard', 'side'))
The draws below stay inside these ranges and needn't reach their ends.
Inputs may be any that keep to these rules, and one draw needn't show every extreme that they name: `routes`: each row names 8 different experts; no expert is named by more than 128 rows, a bound that some block reaches; every expert is named by some row.
All inputs are finite; a program needn't handle non-finite values.
Results may differ from the reference program's by a relative error of at most 0.02.
Values may be sent and summed in bfloat16 or wider, within the bound.
A program may use at most 128 MiB of HBM per device.

```python
import math
import jax
import jax.numpy as jnp
import numpy as np
from jax import lax

D = 2048
F = 768
TOP = 8
NS_ITERS = 5
CAP = 128
EXPERTS = 64
TOKENS = 512


def block_scale(key, dims, pieces, low, high):
    def one(axis_at, parts):
        heights = jax.random.uniform(jax.random.fold_in(jax.random.fold_in(key, 6), axis_at), (parts,), jnp.float32, low / len(pieces), high / len(pieces))
        return jnp.repeat(jnp.exp(heights), dims[axis_at] // parts).reshape((-1,) + (1,) * (len(dims) - axis_at - 1))

    factor_of = one(*pieces[0])
    for cut in pieces[1:]:
        factor_of = factor_of * one(*cut)
    return factor_of


def shared_out(rng, own, number, rows, count, top, most, slope):
    ranking = jax.random.permutation(rng, count)
    crowded, usual = portions_of(count, rows * top, most, slope, True), portions_of(count, rows * top, most, slope, False)
    places = jnp.arange(count)

    def named(tallies, turn):
        used = int((tallies > 0).sum())
        fixed = max(1, used // 4)
        passed = fixed + (places - fixed + turn * (used - fixed)) % max(1, count - fixed)
        return jnp.zeros((count,), jnp.int32).at[ranking[jnp.where(places < fixed, places, passed)]].set(jnp.asarray(tallies, jnp.int32))

    tallies = jnp.where(number % 4 == 0, named(crowded, number // 4), named(usual, number - number // 4 - 1))
    mixed = jax.random.permutation(jax.random.fold_in(own, 3), count)
    source_of, taker = mixed[0:count // 2 * 2:2], mixed[1:count // 2 * 2:2]
    room = jnp.minimum(tallies[source_of] - 1, most - tallies[taker]) // 2
    room = jnp.where((source_of == ranking[0]) | (taker == ranking[0]) | (tallies[taker] == 0), 0, jnp.maximum(room, 0))
    passed = jax.random.randint(jax.random.fold_in(own, 4), (count // 2,), 0, 1 << 20) % (room + 1)
    tallies = tallies.at[source_of].add(-passed).at[taker].add(passed)
    labels = jnp.searchsorted(jnp.cumsum(tallies), jnp.arange(rows * top), side="right").astype(jnp.int32)
    table = labels.reshape(top, rows).T
    table = table[jax.random.permutation(jax.random.fold_in(own, 1), rows)]
    turn = jax.random.randint(jax.random.fold_in(own, 2), (rows, 1), 0, top)
    return jnp.take_along_axis(table, (jnp.arange(top)[None, :] + turn) % top, axis=1)


def portions_of(count, total, reach, skew, full):
    portions = [(1 << 20) // math.isqrt(standing ** skew) + 1 for standing in range(1, count + 1)]
    largest = reach if full else min(reach, max(-(-total // count), total * portions[0] // sum(portions)))
    least = 1 if total - largest >= count - 1 else 0
    holding, rest = [largest] + [least] * (count - 1), total - largest - least * (count - 1)
    while rest > 0:
        free = [i for i in range(1, count) if holding[i] < largest] or [i for i in range(1, count) if holding[i] < reach]
        whole, budget = sum([portions[i] for i in free]), rest
        for i in free:
            extra = min(reach - holding[i], max(1, budget * portions[i] // whole), rest)
            holding[i] = holding[i] + extra
            rest = rest - extra
    return np.array(holding)


def normal_values(rng, extent, spread, most, pieces=(), kind=jnp.bfloat16):
    factor_of = block_scale(rng, extent, pieces, -0.22, 0.18) if pieces else 1.0
    values = jax.random.normal(rng, extent, jnp.float32) * spread * factor_of
    return jnp.minimum(jnp.maximum(values, -most), most).astype(kind)


def setup_inputs(seed: int = 0) -> dict:
    splits = jax.random.split(jax.random.key(seed), 9)
    master = normal_values(splits[0], (EXPERTS, D, F), D ** -0.5, 0.125, ((0, 8), (1, 16)), jnp.float32)
    momentum = normal_values(splits[1], (EXPERTS, D, F), 4.0, 24.0, ((0, 8), (1, 16)), jnp.float32)
    gradient = normal_values(splits[2], (EXPERTS, D, F), 1.0, 6.0, ((0, 8), (1, 16)))
    up_weight = normal_values(splits[3], (EXPERTS, F, D), D ** -0.5, 0.125, ((0, 64), (1, 2)))
    down_weight = normal_values(splits[4], (EXPERTS, F, D), F ** -0.5, 0.21875, ((0, 64), (1, 2)))
    tokens = normal_values(splits[5], (TOKENS, D), 1.0, 6.0)
    routes_keys = jax.random.split(jax.random.fold_in(splits[6], 1), TOKENS // TOKENS)
    routes_turns = jax.random.permutation(jax.random.fold_in(splits[6], 3), TOKENS // TOKENS)
    routes = jax.vmap(lambda own, number: shared_out(jax.random.fold_in(splits[6], 2), own, number, TOKENS, EXPERTS, TOP, CAP, 2))(routes_keys, routes_turns).reshape((TOKENS, TOP))
    route_weight = jnp.clip(jax.random.uniform(splits[7], (TOKENS, TOP), jnp.float32, 0.1, 1.0), 0.1, 1.0)
    return dict(master=master, momentum=momentum, gradient=gradient, up_weight=up_weight, down_weight=down_weight, tokens=tokens, routes=routes, route_weight=route_weight)


MOMENTUM_BETA = 0.95
LEARN_RATE = 0.08
WEIGHT_DECAY = 0.1
NEWTON_A = 3.4445
NEWTON_B = -4.775
NEWTON_C = 2.0315
EPSILON = 1e-07

def orthogonal(blended):
    values = blended.astype(jnp.float32)
    scale_sum = jnp.sqrt(jnp.sum(values * values))
    current = (values / (scale_sum + EPSILON)).astype(jnp.bfloat16)
    for iteration in range(NS_ITERS):
        wide = current.astype(jnp.float32)
        gram_matrix = jnp.dot(wide.T, wide, preferred_element_type=jnp.float32).astype(jnp.bfloat16)
        gram_wide = gram_matrix.astype(jnp.float32)
        square = jnp.dot(gram_wide, gram_wide, preferred_element_type=jnp.float32)
        mixing = (NEWTON_B * gram_wide + NEWTON_C * square).astype(jnp.bfloat16)
        current = (NEWTON_A * wide + jnp.dot(wide, mixing.astype(jnp.float32), preferred_element_type=jnp.float32)).astype(jnp.bfloat16)
    return current

def reference(master, momentum, gradient, up_weight, down_weight, tokens, routes, route_weight):
    new_momentum = MOMENTUM_BETA * momentum + gradient.astype(jnp.float32)
    blended = (gradient.astype(jnp.float32) + MOMENTUM_BETA * new_momentum).astype(jnp.bfloat16)
    updates = lax.map(orthogonal, blended)
    step_scale = LEARN_RATE * 0.2 * math.sqrt(max(D, F))
    new_master = master * (1.0 - LEARN_RATE * WEIGHT_DECAY) - step_scale * updates.astype(jnp.float32)
    live_gate = new_master.astype(jnp.bfloat16)
    positions = jnp.arange(TOKENS, dtype=jnp.int32)

    def expert_step(totals, inputs):
        gate_matrix, up_matrix, down_matrix, expert = inputs
        matches = routes == expert
        member = jnp.any(matches, axis=1)
        weights = lax.optimization_barrier(jnp.sum(jnp.where(matches, route_weight, 0.0), axis=1))
        ordering = jnp.argsort(jnp.where(member, positions, positions + TOKENS))[:CAP].astype(jnp.int32)
        picked = tokens[ordering]
        slot_weight = weights[ordering]
        gate_value = jnp.dot(picked, gate_matrix, preferred_element_type=jnp.float32)
        upward = jnp.dot(picked, up_matrix.T, preferred_element_type=jnp.float32)
        hidden = (jax.nn.silu(gate_value) * upward).astype(jnp.bfloat16)
        output = jnp.dot(hidden, down_matrix, preferred_element_type=jnp.float32)
        totals = totals.at[ordering].add(output * slot_weight[:, None])
        return (totals, None)
    start_totals = jnp.zeros((TOKENS, D), jnp.float32)
    expert_ids = jnp.arange(EXPERTS, dtype=jnp.int32)
    totals, unused = lax.scan(expert_step, start_totals, (live_gate, up_weight, down_weight, expert_ids))
    return (new_master, new_momentum, totals.astype(jnp.bfloat16))
```

```python
import functools
import math

import jax
import jax.numpy as jnp
from jax import lax
from jax.experimental import pallas as pl
from jax.experimental.pallas import tpu as pltpu
from jax.sharding import PartitionSpec as P

NS_ITERS = 5
CAP = 128
MOMENTUM_BETA = 0.95
LEARN_RATE = 0.08
WEIGHT_DECAY = 0.1
NEWTON_A = 3.4445
NEWTON_B = -4.775
NEWTON_C = 2.0315
EPSILON = 1e-07
MESH = pl.DeviceIdType.MESH
F32 = jnp.float32
BF16 = jnp.bfloat16


def dot(a, b):
    return jnp.dot(a, b, preferred_element_type=F32)


def kernel(
    dims,
    master, momentum, gradient, up_hbm, down_hbm, tokens_hbm, routes, route_weight,
    out_master, out_momentum, out_combined,
    mom, grad, mast, sbuf, xbuf, mhalf, mbuf, obuf, osend,
    rf, rb, mb, tf, tb, qf, qb, tx, gx, gsend,
    upw, downw, tok, tok_o, tok_r, upv, hid, weight,
    e1own, e1send, e1recv, e2send, e2recv, e3send, e3recv, comb,
    ld_m, ld_g, ld_x, ld_w, st_m, st_x, st_c,
    a_send, a_recv, f_send, f_recv, d_send, d_recv, c_send, c_recv,
    t_send, t_recv, e1_s, e1_r, e2_s, e2_r, e3_s, e3_r,
):
    NZ, NS, ROWS, F, D, T = dims
    H = F // 2
    NP = 2 * NS
    TB = T // (2 * NZ)
    RB = TB // NP
    gi = lax.axis_index("group")
    z, k = gi // 2, gi % 2
    s = lax.axis_index("shard")
    a = lax.axis_index("side")
    same = a == k
    differ = a != k
    mine = s * 2 + a
    pgroup, pside = z * 2 + a, k
    sibling = {"group": z * 2 + 1 - k, "shard": s, "side": a}
    swap = {"group": z * 2 + 1 - k, "shard": s, "side": 1 - a}

    def remote(src, dst, send, recv, device):
        return pltpu.make_async_remote_copy(
            src_ref=src, dst_ref=dst, send_sem=send, recv_sem=recv,
            device_id=device, device_id_type=MESH,
        )

    def rows_of(r):
        return pl.ds(pl.multiple_of(r * ROWS, ROWS), ROWS)

    def load(j):
        pltpu.make_async_copy(momentum.at[j], mom.at[j], ld_m.at[j]).start()
        pltpu.make_async_copy(gradient.at[j], grad.at[j], ld_g.at[j]).start()

    def turn(t):
        return lax.rem(s + 1 + t, NS)

    def origin(t):
        return lax.rem(s + 2 * NS - 1 - t, NS)

    @pl.loop(0, NS)
    def _(t):
        load(turn(t))

    w_loads = [
        pltpu.make_async_copy(tokens_hbm, tok, ld_w.at[0]),
        pltpu.make_async_copy(up_hbm.at[0], upw, ld_w.at[1]),
        pltpu.make_async_copy(down_hbm.at[0], downw, ld_w.at[2]),
    ]

    barrier = pltpu.get_barrier_semaphore()

    def greet(device):
        pl.semaphore_signal(barrier, inc=1, device_id=device, device_id_type=MESH)

    @pl.loop(1, NP)
    def _(i):
        r = lax.rem(mine + i, NP)
        greet({"group": gi, "shard": r // 2, "side": lax.rem(r, 2)})

    @pl.loop(1, NZ)
    def _(i):
        greet({"group": lax.rem(z + i, NZ) * 2 + k, "shard": s, "side": a})

    greet(sibling)

    @pl.when(differ)
    def _():
        @pl.loop(0, NS)
        def _(j):
            greet({"group": pgroup, "shard": j, "side": pside})

        pl.semaphore_wait(barrier, NP - 1 + NZ - 1 + 1 + NS)

    @pl.when(same)
    def _():
        pl.semaphore_wait(barrier, NP - 1 + NZ - 1 + 1)

    def a_copy(j):
        return remote(
            sbuf.at[j], xbuf.at[rows_of(mine)], a_send.at[j], a_recv.at[s],
            {"group": pgroup, "shard": j, "side": pside},
        )

    @pl.loop(0, NS)
    def _(t):
        j = turn(t)
        pltpu.make_async_copy(momentum.at[j], mom.at[j], ld_m.at[j]).wait()
        pltpu.make_async_copy(gradient.at[j], grad.at[j], ld_g.at[j]).wait()
        g = grad[j].astype(F32)
        m = MOMENTUM_BETA * mom[j] + g
        mom[j] = m
        sbuf[j] = (g + MOMENTUM_BETA * m).astype(BF16)
        own = jnp.logical_and(same, j == s)

        @pl.when(own)
        def _():
            xbuf[rows_of(mine), :] = sbuf[j]

        @pl.when(jnp.logical_not(own))
        def _():
            a_copy(j).start()

        pltpu.make_async_copy(mom.at[j], out_momentum.at[j], st_m.at[j]).start()

    for c in w_loads:
        c.start()

    @pl.loop(0, NS)
    def _(t):
        j = turn(t)
        pltpu.make_async_copy(master.at[j], mast.at[j], ld_x.at[j]).start()

    for c in w_loads:
        c.wait()
    token_row = lax.broadcasted_iota(jnp.int32, (T, T), 0)
    token_col = lax.broadcasted_iota(jnp.int32, (T, T), 1)
    lower = jnp.where(token_col <= token_row, 1.0, 0.0).astype(BF16)

    def slots(expert):
        hit = routes[...] == expert
        member = jnp.max(jnp.where(hit, 1.0, 0.0), axis=1, keepdims=True)
        wide = jnp.broadcast_to(member, (T, CAP))
        rank = dot(lower, wide.astype(BF16))
        slot = lax.broadcasted_iota(jnp.int32, (T, CAP), 1).astype(F32) + 1.0
        chosen = jnp.where(jnp.logical_and(rank == slot, wide > 0.5), 1.0, 0.0)
        return chosen.astype(BF16), hit

    def pick(chosen):
        return lax.dot_general(
            chosen, tok[...], (((0,), (0,)), ((), ())), preferred_element_type=F32
        ).astype(BF16)

    chosen_o, _ = slots((z * 2 + a) * NS + s)
    tok_o[...] = pick(chosen_o)
    chosen_r, hit_r = slots(gi * NS + s)
    tok_r[...] = pick(chosen_r)
    weight[...] = jnp.broadcast_to(
        jnp.sum(jnp.where(hit_r, route_weight[...], 0.0), axis=1, keepdims=True), (T, 128)
    )
    upv[...] = lax.dot_general(
        tok_r[...], upw[...], (((1,), (1,)), ((), ())), preferred_element_type=F32
    )

    @pl.loop(0, NS)
    def _(t):
        j = turn(t)
        pltpu.make_async_copy(master.at[j], mast.at[j], ld_x.at[j]).wait()
        half = mast[j].astype(BF16)
        mhalf[j, 0] = half[:, :H]
        mhalf[j, 1] = half[:, H:]

    rf[...] = jnp.zeros_like(rf)
    tx[...] = jnp.zeros_like(tx)

    def f_copy(o, core):
        block = rows_of(o * 2 + core)
        return remote(xbuf.at[block], xbuf.at[block], f_send.at[o], f_recv.at[o], sibling)

    def gram(o):
        f_copy(o, 1 - k).wait_recv()
        pair = pl.ds(pl.multiple_of(o * 2 * ROWS, 2 * ROWS), 2 * ROWS)
        x = xbuf[pair, :]
        rf[...] += lax.dot_general(
            x, x, (((0,), (0,)), ((), ())), preferred_element_type=F32
        )
        tx[...] += dot(tok_o[:, pair], x)

    @pl.loop(0, NS)
    def _(t):
        o = origin(t)

        @pl.when(jnp.logical_not(jnp.logical_and(same, o == s)))
        def _():
            remote(
                sbuf.at[o], xbuf.at[rows_of(o * 2 + k)], a_send.at[o], a_recv.at[o],
                {"group": pgroup, "shard": o, "side": pside},
            ).wait_recv()

        f_copy(o, k).start()

        @pl.when(t > 0)
        def _():
            gram(origin(t - 1))

    gram(origin(NS - 1))

    def d_copy(j, h):
        return remote(
            mhalf.at[j, h], mbuf.at[rows_of(mine)], d_send.at[j * 2 + h], d_recv.at[mine],
            {"group": gi, "shard": j, "side": h},
        )

    @pl.loop(0, NP)
    def _(i):
        r = lax.rem(mine + i, NP)
        j, h = r // 2, lax.rem(r, 2)

        @pl.when(i == 0)
        def _():
            mbuf[rows_of(mine), :] = mhalf[j, h]

        @pl.when(i > 0)
        def _():
            d_copy(j, h).start()

    B = 128
    eye = lax.broadcasted_iota(jnp.int32, (B, B), 0) == lax.broadcasted_iota(jnp.int32, (B, B), 1)
    blocks = [pl.ds(i * B, B) for i in range(F // B)]
    halves = [pl.ds(0, H), pl.ds(H, H)]

    def trace_of_rf():
        total = jnp.zeros((B, B), F32)
        for b in blocks:
            total = total + jnp.where(eye, rf[b, b], 0.0)
        return jnp.sum(total)

    def shift_rf(d):
        for b in blocks:
            v = rf[b, b] - jnp.where(eye, d, 0.0)
            rf[b, b] = v
            rb[b, b] = v.astype(BF16)

    scale = jnp.sqrt(trace_of_rf() + jnp.zeros((1, 1), F32))[0, 0]
    inverse = (1.0 / (jnp.zeros((1, 1), F32) + scale + EPSILON))[0, 0]
    for h in halves:
        v = rf[h, :] * inverse * inverse
        rf[h, :] = v
        rb[h, :] = v.astype(BF16)

    def recenter(d):
        move = trace_of_rf() * (1.0 / F)
        shift_rf(move)
        return d + move

    def form_mix(d):
        e1 = NEWTON_B + 2.0 * NEWTON_C * d
        for h in halves:
            mb[h, :] = (e1 * rf[h, :] + NEWTON_C * dot(rb[h, :], rb[...])).astype(BF16)
        return NEWTON_A + NEWTON_B * d + NEWTON_C * d * d

    def grow_q(lead, q):
        for h in halves:
            v = lead * qf[h, :] + q * mb[h, :].astype(F32) + dot(qb[h, :], mb[...])
            qf[h, :] = v
            qb[h, :] = v.astype(BF16)
        return q * lead

    def grow_g(lead, d):
        for h in halves:
            v = lead * rf[h, :] + d * mb[h, :].astype(F32) + dot(rb[h, :], mb[...])
            tf[h, :] = v
            tb[h, :] = v.astype(BF16)
        t = lead * d
        for h in halves:
            v = lead * tf[h, :] + t * mb[h, :].astype(F32) + dot(tb[h, :], mb[...])
            rf[h, :] = v
            rb[h, :] = v.astype(BF16)
        return lead * t

    d = recenter(jnp.float32(0.0))
    lead = form_mix(d)
    q = lead
    qf[...] = mb[...].astype(F32)
    qb[...] = mb[...]
    d = grow_g(lead, d)

    def iteration(_, carry):
        d, q = carry
        d = recenter(d)
        lead = form_mix(d)
        q = grow_q(lead, q)
        d = grow_g(lead, d)
        return d, q

    d, q = lax.fori_loop(1, NS_ITERS - 1, iteration, (d, q))
    d = recenter(d)
    lead = form_mix(d)
    q = grow_q(lead, q)

    cols = pl.ds(pl.multiple_of(k * H, H), H)
    part = inverse * (q * tx[:, cols] + dot(tx[...].astype(BF16), qb[:, cols]))
    t_copy = remote(gsend, gx, t_send, t_recv, swap)

    @pl.when(same)
    def _():
        gx[...] = part.astype(BF16)

    @pl.when(differ)
    def _():
        gsend[...] = part.astype(BF16)
        t_copy.start()

    def c_copy(o):
        return remote(
            osend.at[o], obuf.at[s], c_send.at[o], c_recv.at[s],
            {"group": pgroup, "shard": o, "side": pside},
        )

    BUNCH = min(4, NS)
    for first in range(0, NS, BUNCH):
        who = [turn(first + i) for i in range(BUNCH)]
        x = jnp.concatenate([xbuf[rows_of(o * 2 + k), :] for o in who], axis=0)
        y = (inverse * (q * x.astype(F32) + dot(x, qb[...]))).astype(BF16)
        for i, o in enumerate(who):
            osend[o] = y[i * ROWS:(i + 1) * ROWS]
            own = jnp.logical_and(same, o == s)

            @pl.when(own)
            def _():
                obuf[s] = osend[o]

            @pl.when(jnp.logical_not(own))
            def _():
                c_copy(o).start()

    @pl.loop(1, NP)
    def _(i):
        r = lax.rem(mine + i, NP)
        remote(
            mhalf.at[r // 2, lax.rem(r, 2)], mbuf.at[rows_of(r)], d_send.at[r], d_recv.at[r],
            {"group": gi, "shard": r // 2, "side": lax.rem(r, 2)},
        ).wait_recv()

    decay = 1.0 - LEARN_RATE * WEIGHT_DECAY
    step_scale = LEARN_RATE * 0.2 * math.sqrt(max(D, F))
    kept = decay * dot(tok_r[...], mbuf[...])

    @pl.when(differ)
    def _():
        t_copy.wait_recv()

    gate = kept - step_scale * gx[...].astype(F32)
    hidden = (gate * (1.0 / (1.0 + jnp.exp(-gate))) * upv[...]).astype(BF16)
    hid[...] = dot(chosen_r, hidden).astype(BF16)

    def share(core):
        parts = [pl.ds(pl.multiple_of((i * 2 + core) * TB, TB), TB) for i in range(NZ)]
        rows = jnp.concatenate([hid[p, :] for p in parts], axis=0)
        value = dot(rows, downw[...])
        scale = jnp.concatenate([weight[p, :1] for p in parts], axis=0)
        return value * scale

    away = share(1 - k).astype(BF16)
    for i in range(NZ):
        e1send[i] = away[i * TB:(i + 1) * TB]
    e1_copy = remote(e1send, e1recv, e1_s, e1_r, sibling)
    e1_copy.start()
    home = share(k)
    for i in range(NZ):
        e1own[i] = home[i * TB:(i + 1) * TB]
    e1_copy.wait_recv()

    def e2_copy(i):
        return remote(
            e2send.at[i], e2recv.at[i], e2_s.at[i], e2_r.at[i],
            {"group": lax.rem(z + 1 + i, NZ) * 2 + k, "shard": s, "side": a},
        )

    @pl.loop(0, NZ - 1)
    def _(i):
        to = lax.rem(z + 1 + i, NZ)
        e2send[i] = (e1own[to] + e1recv[to].astype(F32)).astype(BF16)
        e2_copy(i).start()

    total = e1own[z] + e1recv[z].astype(F32)
    for i in range(NZ - 1):
        e2_copy(i).wait_recv()
        total = total + e2recv[i].astype(F32)
    for r in range(NP):
        e3send[r] = total[r * RB:(r + 1) * RB].astype(BF16)

    def e3_copy(r, slot):
        return remote(
            e3send.at[r], e3recv.at[slot], e3_s.at[r], e3_r.at[slot],
            {"group": gi, "shard": r // 2, "side": lax.rem(r, 2)},
        )

    @pl.loop(1, NP)
    def _(i):
        e3_copy(lax.rem(mine + i, NP), mine).start()

    e3recv[mine] = e3send[mine]

    @pl.loop(0, NS)
    def _(t):
        o = origin(t)

        @pl.when(jnp.logical_not(jnp.logical_and(same, o == s)))
        def _():
            remote(
                osend.at[o], obuf.at[o], c_send.at[o], c_recv.at[o],
                {"group": pgroup, "shard": o, "side": pside},
            ).wait_recv()

        mast[o] = decay * mast[o] - step_scale * obuf[o].astype(F32)
        pltpu.make_async_copy(mast.at[o], out_master.at[o], st_x.at[o]).start()

    @pl.loop(1, NP)
    def _(i):
        r = lax.rem(mine + i, NP)
        e3_copy(r, r).wait_recv()

    final = e3recv[0].astype(F32)
    for r in range(1, NP):
        final = final + e3recv[r].astype(F32)
    comb[...] = final.astype(BF16)
    last = pltpu.make_async_copy(comb, out_combined, st_c)
    last.start()

    @pl.loop(0, NS)
    def _(t):
        j = turn(t)

        @pl.when(jnp.logical_not(jnp.logical_and(same, j == s)))
        def _():
            a_copy(j).wait_send()
            c_copy(j).wait_send()

        f_copy(j, k).wait_send()
        pltpu.make_async_copy(mom.at[j], out_momentum.at[j], st_m.at[j]).wait()
        pltpu.make_async_copy(mast.at[j], out_master.at[j], st_x.at[j]).wait()

    @pl.loop(1, NP)
    def _(i):
        r = lax.rem(mine + i, NP)
        d_copy(r // 2, lax.rem(r, 2)).wait_send()
        e3_copy(r, mine).wait_send()

    @pl.loop(0, NZ - 1)
    def _(i):
        e2_copy(i).wait_send()

    e1_copy.wait_send()

    @pl.when(differ)
    def _():
        t_copy.wait_send()

    last.wait()


def body(master, momentum, gradient, up_weight, down_weight, tokens, routes, route_weight):
    NS, ROWS, F = master.shape
    NZ = lax.axis_size("group") // 2
    T, D = tokens.shape
    H = F // 2
    NP = 2 * NS
    TB = T // (2 * NZ)
    RB = TB // NP
    dma = pltpu.SemaphoreType.DMA
    vmem = pltpu.VMEM
    scratch = dict(
        mom=vmem((NS, ROWS, F), F32), grad=vmem((NS, ROWS, F), BF16), mast=vmem((NS, ROWS, F), F32),
        sbuf=vmem((NS, ROWS, F), BF16), xbuf=vmem((D, F), BF16), mhalf=vmem((NS, 2, ROWS, H), BF16),
        mbuf=vmem((D, H), BF16), obuf=vmem((NS, ROWS, F), BF16), osend=vmem((NS, ROWS, F), BF16),
        rf=vmem((F, F), F32), rb=vmem((F, F), BF16), mb=vmem((F, F), BF16), tf=vmem((F, F), F32),
        tb=vmem((F, F), BF16), qf=vmem((F, F), F32), qb=vmem((F, F), BF16), tx=vmem((CAP, F), F32),
        gx=vmem((CAP, H), BF16), gsend=vmem((CAP, H), BF16),
        upw=vmem((H, D), BF16), downw=vmem((H, D), BF16), tok=vmem((T, D), BF16),
        tok_o=vmem((CAP, D), BF16), tok_r=vmem((CAP, D), BF16), upv=vmem((CAP, H), F32),
        hid=vmem((T, H), BF16), weight=vmem((T, 128), F32),
        e1own=vmem((NZ, TB, D), F32), e1send=vmem((NZ, TB, D), BF16), e1recv=vmem((NZ, TB, D), BF16),
        e2send=vmem((NZ - 1, TB, D), BF16), e2recv=vmem((NZ - 1, TB, D), BF16),
        e3send=vmem((NP, RB, D), BF16), e3recv=vmem((NP, RB, D), BF16), comb=vmem((RB, D), BF16),
        ld_m=dma((NS,)), ld_g=dma((NS,)), ld_x=dma((NS,)), ld_w=dma((3,)),
        st_m=dma((NS,)), st_x=dma((NS,)), st_c=dma,
        a_send=dma((NS,)), a_recv=dma((NS,)), f_send=dma((NS,)), f_recv=dma((NS,)),
        d_send=dma((NP,)), d_recv=dma((NP,)), c_send=dma((NS,)), c_recv=dma((NS,)),
        t_send=dma, t_recv=dma, e1_s=dma, e1_r=dma,
        e2_s=dma((NZ - 1,)), e2_r=dma((NZ - 1,)), e3_s=dma((NP,)), e3_r=dma((NP,)),
    )
    hbm = pl.BlockSpec(memory_space=pl.ANY)
    local = pl.BlockSpec(memory_space=pltpu.VMEM)
    return pl.pallas_call(
        functools.partial(kernel, (NZ, NS, ROWS, F, D, T)),
        out_shape=(
            jax.ShapeDtypeStruct(master.shape, F32),
            jax.ShapeDtypeStruct(master.shape, F32),
            jax.ShapeDtypeStruct((RB, D), BF16),
        ),
        in_specs=[hbm] * 6 + [local] * 2,
        out_specs=[hbm] * 3,
        scratch_shapes=list(scratch.values()),
        compiler_params=pltpu.CompilerParams(
            collective_id=0, has_side_effects=True, vmem_limit_bytes=60 * 1024 * 1024
        ),
        name="muon_rollout",
    )(master, momentum, gradient, up_weight, down_weight, tokens, routes, route_weight)


def solution(mesh):
    in_specs = (
        P("group", ("shard", "side"), None),
        P("group", ("shard", "side"), None),
        P("group", ("shard", "side"), None),
        P(("group", "shard"), "side", None),
        P(("group", "shard"), "side", None),
        P(),
        P(),
        P(),
    )
    out_specs = (
        P("group", ("shard", "side"), None),
        P("group", ("shard", "side"), None),
        P(("group", "shard", "side"), None),
    )
    return jax.shard_map(body, mesh=mesh, in_specs=in_specs, out_specs=out_specs, check_vma=False)
```

```python
import functools
import math

import jax
import jax.numpy as jnp
from jax import lax
from jax.experimental import pallas as pl
from jax.experimental.pallas import tpu as pltpu
from jax.sharding import PartitionSpec as P

NS_ITERS = 5
CAP = 128
MOMENTUM_BETA = 0.95
LEARN_RATE = 0.08
WEIGHT_DECAY = 0.1
NEWTON_A = 3.4445
NEWTON_B = -4.775
NEWTON_C = 2.0315
EPSILON = 1e-07
MESH = pl.DeviceIdType.MESH
F32 = jnp.float32
BF16 = jnp.bfloat16


def dot(a, b):
    return jnp.dot(a, b, preferred_element_type=F32)


def kernel(
    dims,
    master, momentum, gradient, up_hbm, down_hbm, tokens_hbm, routes, route_weight,
    mast, mom, comb,
    grad, sbuf, xbuf, mhalf, mbuf, obuf, osend,
    rf, rb, mb, tf, tb, qf, qb, tx, gx, gsend,
    upw, downw, tok, tok_o, tok_r, upv, hid, chosen,
    e1own, e1send, e1recv, e2send, e2recv, e3send, e3recv,
    ld_m, ld_g, ld_x, ld_w,
    a_send, a_recv, f_send, f_recv, d_send, d_recv, c_send, c_recv,
    t_send, t_recv, e1_s, e1_r, e2_s, e2_r, e3_s, e3_r,
):
    NZ, NS, ROWS, F, D, T = dims
    H = F // 2
    NP = 2 * NS
    TB = T // (2 * NZ)
    RB = TB // NP
    gi = lax.axis_index("group")
    z, k = gi // 2, gi % 2
    s = lax.axis_index("shard")
    a = lax.axis_index("side")
    same = a == k
    differ = a != k
    mine = s * 2 + a
    pgroup, pside = z * 2 + a, k
    sibling = {"group": z * 2 + 1 - k, "shard": s, "side": a}
    swap = {"group": z * 2 + 1 - k, "shard": s, "side": 1 - a}

    def remote(src, dst, send, recv, device):
        return pltpu.make_async_remote_copy(
            src_ref=src, dst_ref=dst, send_sem=send, recv_sem=recv,
            device_id=device, device_id_type=MESH,
        )

    def rows_of(r):
        return pl.ds(pl.multiple_of(r * ROWS, ROWS), ROWS)

    def load(j):
        pltpu.make_async_copy(momentum.at[j], mom.at[j], ld_m.at[j]).start()
        pltpu.make_async_copy(gradient.at[j], grad.at[j], ld_g.at[j]).start()

    def turn(t):
        return lax.rem(s + 1 + t, NS)

    def origin(t):
        return lax.rem(s + 2 * NS - 1 - t, NS)

    @pl.loop(0, NS)
    def _(t):
        load(turn(t))

    w_loads = [
        pltpu.make_async_copy(tokens_hbm, tok, ld_w.at[0]),
        pltpu.make_async_copy(up_hbm.at[0], upw, ld_w.at[1]),
        pltpu.make_async_copy(down_hbm.at[0], downw, ld_w.at[2]),
    ]

    barrier = pltpu.get_barrier_semaphore()

    def greet(device):
        pl.semaphore_signal(barrier, inc=1, device_id=device, device_id_type=MESH)

    @pl.loop(1, NP)
    def _(i):
        r = lax.rem(mine + i, NP)
        greet({"group": gi, "shard": r // 2, "side": lax.rem(r, 2)})

    @pl.loop(1, NZ)
    def _(i):
        greet({"group": lax.rem(z + i, NZ) * 2 + k, "shard": s, "side": a})

    greet(sibling)

    @pl.when(differ)
    def _():
        @pl.loop(0, NS)
        def _(j):
            greet({"group": pgroup, "shard": j, "side": pside})

        pl.semaphore_wait(barrier, NP - 1 + NZ - 1 + 1 + NS)

    @pl.when(same)
    def _():
        pl.semaphore_wait(barrier, NP - 1 + NZ - 1 + 1)

    def a_copy(j):
        return remote(
            sbuf.at[j], xbuf.at[rows_of(mine)], a_send.at[j], a_recv.at[s],
            {"group": pgroup, "shard": j, "side": pside},
        )

    @pl.loop(0, NS)
    def _(t):
        j = turn(t)
        pltpu.make_async_copy(momentum.at[j], mom.at[j], ld_m.at[j]).wait()
        pltpu.make_async_copy(gradient.at[j], grad.at[j], ld_g.at[j]).wait()
        g = grad[j].astype(F32)
        m = MOMENTUM_BETA * mom[j] + g
        mom[j] = m
        sbuf[j] = (g + MOMENTUM_BETA * m).astype(BF16)
        own = jnp.logical_and(same, j == s)

        @pl.when(own)
        def _():
            xbuf[rows_of(mine), :] = sbuf[j]

        @pl.when(jnp.logical_not(own))
        def _():
            a_copy(j).start()

    for c in w_loads:
        c.start()

    @pl.loop(0, NS)
    def _(t):
        j = turn(t)
        pltpu.make_async_copy(master.at[j], mast.at[j], ld_x.at[j]).start()

    for c in w_loads:
        c.wait()
    token_row = lax.broadcasted_iota(jnp.int32, (T, T), 0)
    token_col = lax.broadcasted_iota(jnp.int32, (T, T), 1)
    upper = jnp.where(token_row <= token_col, 1.0, 0.0).astype(BF16)

    def slots(expert):
        hit = routes[...] == expert
        member = jnp.max(jnp.where(hit, 1.0, 0.0), axis=0, keepdims=True)
        rank = dot(jnp.broadcast_to(member, (16, T)).astype(BF16), upper)[:1]
        place = jnp.where(member > 0.5, rank - 1.0, -1.0)
        slot = lax.broadcasted_iota(jnp.int32, (CAP, T), 0).astype(F32)
        return jnp.where(slot == place, 1.0, 0.0), hit

    chosen_o, _ = slots((z * 2 + a) * NS + s)
    tok_o[...] = dot(chosen_o.astype(BF16), tok[...]).astype(BF16)
    chosen_r, hit_r = slots(gi * NS + s)
    tok_r[...] = dot(chosen_r.astype(BF16), tok[...]).astype(BF16)
    weight = jnp.sum(jnp.where(hit_r, route_weight[...], 0.0), axis=0, keepdims=True)
    weight = jnp.sum(chosen_r * weight, axis=1, keepdims=True)
    chosen[...] = chosen_r.astype(BF16)
    upv[...] = weight * lax.dot_general(
        tok_r[...], upw[...], (((1,), (1,)), ((), ())), preferred_element_type=F32
    )

    @pl.loop(0, NS)
    def _(t):
        j = turn(t)
        pltpu.make_async_copy(master.at[j], mast.at[j], ld_x.at[j]).wait()
        half = mast[j].astype(BF16)
        mhalf[j, 0] = half[:, :H]
        mhalf[j, 1] = half[:, H:]

    rf[...] = jnp.zeros_like(rf)
    tx[...] = jnp.zeros_like(tx)

    def f_copy(o, core):
        block = rows_of(o * 2 + core)
        return remote(xbuf.at[block], xbuf.at[block], f_send.at[o], f_recv.at[o], sibling)

    def gram(o):
        f_copy(o, 1 - k).wait_recv()
        pair = pl.ds(pl.multiple_of(o * 2 * ROWS, 2 * ROWS), 2 * ROWS)
        x = xbuf[pair, :]
        rf[...] += lax.dot_general(
            x, x, (((0,), (0,)), ((), ())), preferred_element_type=F32
        )
        tx[...] += dot(tok_o[:, pair], x)

    @pl.loop(0, NS)
    def _(t):
        o = origin(t)

        @pl.when(jnp.logical_not(jnp.logical_and(same, o == s)))
        def _():
            remote(
                sbuf.at[o], xbuf.at[rows_of(o * 2 + k)], a_send.at[o], a_recv.at[o],
                {"group": pgroup, "shard": o, "side": pside},
            ).wait_recv()

        f_copy(o, k).start()

        @pl.when(t > 0)
        def _():
            gram(origin(t - 1))

    gram(origin(NS - 1))

    def d_copy(j, h):
        return remote(
            mhalf.at[j, h], mbuf.at[rows_of(mine)], d_send.at[j * 2 + h], d_recv.at[mine],
            {"group": gi, "shard": j, "side": h},
        )

    @pl.loop(0, NP)
    def _(i):
        r = lax.rem(mine + i, NP)
        j, h = r // 2, lax.rem(r, 2)

        @pl.when(i == 0)
        def _():
            mbuf[rows_of(mine), :] = mhalf[j, h]

        @pl.when(i > 0)
        def _():
            d_copy(j, h).start()

    B = 128
    eye = lax.broadcasted_iota(jnp.int32, (B, B), 0) == lax.broadcasted_iota(jnp.int32, (B, B), 1)
    blocks = [pl.ds(i * B, B) for i in range(F // B)]
    halves = [pl.ds(0, H), pl.ds(H, H)]

    def trace_of_rf():
        total = jnp.zeros((B, B), F32)
        for b in blocks:
            total = total + jnp.where(eye, rf[b, b], 0.0)
        return jnp.sum(total)

    def shift_rf(d):
        for b in blocks:
            v = rf[b, b] - jnp.where(eye, d, 0.0)
            rf[b, b] = v
            rb[b, b] = v.astype(BF16)

    scale = jnp.sqrt(trace_of_rf() + jnp.zeros((1, 1), F32))[0, 0]
    inverse = (1.0 / (jnp.zeros((1, 1), F32) + scale + EPSILON))[0, 0]
    for h in halves:
        v = rf[h, :] * inverse * inverse
        rf[h, :] = v
        rb[h, :] = v.astype(BF16)

    def recenter(d):
        move = trace_of_rf() * (1.0 / F)
        shift_rf(move)
        return d + move

    def form_mix(d):
        e1 = NEWTON_B + 2.0 * NEWTON_C * d
        for h in halves:
            mb[h, :] = (e1 * rf[h, :] + NEWTON_C * dot(rb[h, :], rb[...])).astype(BF16)
        return NEWTON_A + NEWTON_B * d + NEWTON_C * d * d

    def grow_q(lead, q):
        for h in halves:
            v = lead * qf[h, :] + q * mb[h, :].astype(F32) + dot(qb[h, :], mb[...])
            qf[h, :] = v
            qb[h, :] = v.astype(BF16)
        return q * lead

    def grow_g(lead, d):
        for h in halves:
            v = lead * rf[h, :] + d * mb[h, :].astype(F32) + dot(rb[h, :], mb[...])
            tf[h, :] = v
            tb[h, :] = v.astype(BF16)
        t = lead * d
        for h in halves:
            v = lead * tf[h, :] + t * mb[h, :].astype(F32) + dot(tb[h, :], mb[...])
            rf[h, :] = v
            rb[h, :] = v.astype(BF16)
        return lead * t

    d = recenter(jnp.float32(0.0))
    lead = form_mix(d)
    q = lead
    qf[...] = mb[...].astype(F32)
    qb[...] = mb[...]
    d = grow_g(lead, d)

    def iteration(_, carry):
        d, q = carry
        d = recenter(d)
        lead = form_mix(d)
        q = grow_q(lead, q)
        d = grow_g(lead, d)
        return d, q

    d, q = lax.fori_loop(1, NS_ITERS - 1, iteration, (d, q))
    d = recenter(d)
    lead = form_mix(d)
    q = grow_q(lead, q)

    cols = pl.ds(pl.multiple_of(k * H, H), H)
    part = inverse * (q * tx[:, cols] + dot(tx[...].astype(BF16), qb[:, cols]))
    t_copy = remote(gsend, gx, t_send, t_recv, swap)

    @pl.when(same)
    def _():
        gx[...] = part.astype(BF16)

    @pl.when(differ)
    def _():
        gsend[...] = part.astype(BF16)
        t_copy.start()

    def c_copy(o):
        return remote(
            osend.at[o], obuf.at[s], c_send.at[o], c_recv.at[s],
            {"group": pgroup, "shard": o, "side": pside},
        )

    BUNCH = min(4, NS)
    for first in range(0, NS, BUNCH):
        who = [turn(first + i) for i in range(BUNCH)]
        x = jnp.concatenate([xbuf[rows_of(o * 2 + k), :] for o in who], axis=0)
        y = (inverse * (q * x.astype(F32) + dot(x, qb[...]))).astype(BF16)
        for i, o in enumerate(who):
            osend[o] = y[i * ROWS:(i + 1) * ROWS]
            own = jnp.logical_and(same, o == s)

            @pl.when(own)
            def _():
                obuf[s] = osend[o]

            @pl.when(jnp.logical_not(own))
            def _():
                c_copy(o).start()

    @pl.loop(1, NP)
    def _(i):
        r = lax.rem(mine + i, NP)
        remote(
            mhalf.at[r // 2, lax.rem(r, 2)], mbuf.at[rows_of(r)], d_send.at[r], d_recv.at[r],
            {"group": gi, "shard": r // 2, "side": lax.rem(r, 2)},
        ).wait_recv()

    decay = 1.0 - LEARN_RATE * WEIGHT_DECAY
    step_scale = LEARN_RATE * 0.2 * math.sqrt(max(D, F))
    kept = decay * dot(tok_r[...], mbuf[...])

    @pl.when(differ)
    def _():
        t_copy.wait_recv()

    gate = kept - step_scale * gx[...].astype(F32)
    hidden = (gate * (1.0 / (1.0 + jnp.exp(-gate))) * upv[...]).astype(BF16)
    hid[...] = lax.dot_general(
        chosen[...], hidden, (((0,), (0,)), ((), ())), preferred_element_type=F32
    ).astype(BF16)

    def share(core):
        parts = [pl.ds(pl.multiple_of((i * 2 + core) * TB, TB), TB) for i in range(NZ)]
        rows = jnp.concatenate([hid[p, :] for p in parts], axis=0)
        return dot(rows, downw[...])

    away = share(1 - k).astype(BF16)
    for i in range(NZ):
        e1send[i] = away[i * TB:(i + 1) * TB]
    e1_copy = remote(e1send, e1recv, e1_s, e1_r, sibling)
    e1_copy.start()
    home = share(k)
    for i in range(NZ):
        e1own[i] = home[i * TB:(i + 1) * TB]
    e1_copy.wait_recv()

    def e2_copy(i):
        return remote(
            e2send.at[i], e2recv.at[i], e2_s.at[i], e2_r.at[i],
            {"group": lax.rem(z + 1 + i, NZ) * 2 + k, "shard": s, "side": a},
        )

    @pl.loop(0, NZ - 1)
    def _(i):
        to = lax.rem(z + 1 + i, NZ)
        e2send[i] = (e1own[to] + e1recv[to].astype(F32)).astype(BF16)
        e2_copy(i).start()

    total = e1own[z] + e1recv[z].astype(F32)
    for i in range(NZ - 1):
        e2_copy(i).wait_recv()
        total = total + e2recv[i].astype(F32)
    for r in range(NP):
        e3send[r] = total[r * RB:(r + 1) * RB].astype(BF16)

    def e3_copy(r, slot):
        return remote(
            e3send.at[r], e3recv.at[slot], e3_s.at[r], e3_r.at[slot],
            {"group": gi, "shard": r // 2, "side": lax.rem(r, 2)},
        )

    @pl.loop(1, NP)
    def _(i):
        e3_copy(lax.rem(mine + i, NP), mine).start()

    e3recv[mine] = e3send[mine]

    @pl.loop(0, NS)
    def _(t):
        o = origin(t)

        @pl.when(jnp.logical_not(jnp.logical_and(same, o == s)))
        def _():
            remote(
                osend.at[o], obuf.at[o], c_send.at[o], c_recv.at[o],
                {"group": pgroup, "shard": o, "side": pside},
            ).wait_recv()

        mast[o] = decay * mast[o] - step_scale * obuf[o].astype(F32)

    @pl.loop(1, NP)
    def _(i):
        r = lax.rem(mine + i, NP)
        e3_copy(r, r).wait_recv()

    final = e3recv[0].astype(F32)
    for r in range(1, NP):
        final = final + e3recv[r].astype(F32)
    comb[...] = final.astype(BF16)

    @pl.loop(0, NS)
    def _(t):
        j = turn(t)

        @pl.when(jnp.logical_not(jnp.logical_and(same, j == s)))
        def _():
            a_copy(j).wait_send()
            c_copy(j).wait_send()

        f_copy(j, k).wait_send()

    @pl.loop(1, NP)
    def _(i):
        r = lax.rem(mine + i, NP)
        d_copy(r // 2, lax.rem(r, 2)).wait_send()
        e3_copy(r, mine).wait_send()

    @pl.loop(0, NZ - 1)
    def _(i):
        e2_copy(i).wait_send()

    e1_copy.wait_send()

    @pl.when(differ)
    def _():
        t_copy.wait_send()


def hand_over(*refs):
    copies = [pltpu.make_async_copy(refs[i], refs[3 + i], refs[6].at[i]) for i in range(3)]
    for c in copies:
        c.start()
    for c in copies:
        c.wait()


def body(master, momentum, gradient, up_weight, down_weight, tokens, routes, route_weight):
    NS, ROWS, F = master.shape
    NZ = lax.axis_size("group") // 2
    T, D = tokens.shape
    H = F // 2
    NP = 2 * NS
    TB = T // (2 * NZ)
    RB = TB // NP
    dma = pltpu.SemaphoreType.DMA
    vmem = pltpu.VMEM
    scratch = dict(
        grad=vmem((NS, ROWS, F), BF16),
        sbuf=vmem((NS, ROWS, F), BF16), xbuf=vmem((D, F), BF16), mhalf=vmem((NS, 2, ROWS, H), BF16),
        mbuf=vmem((D, H), BF16), obuf=vmem((NS, ROWS, F), BF16), osend=vmem((NS, ROWS, F), BF16),
        rf=vmem((F, F), F32), rb=vmem((F, F), BF16), mb=vmem((F, F), BF16), tf=vmem((F, F), F32),
        tb=vmem((F, F), BF16), qf=vmem((F, F), F32), qb=vmem((F, F), BF16), tx=vmem((CAP, F), F32),
        gx=vmem((CAP, H), BF16), gsend=vmem((CAP, H), BF16),
        upw=vmem((H, D), BF16), downw=vmem((H, D), BF16), tok=vmem((T, D), BF16),
        tok_o=vmem((CAP, D), BF16), tok_r=vmem((CAP, D), BF16), upv=vmem((CAP, H), F32),
        hid=vmem((T, H), BF16), chosen=vmem((CAP, T), BF16),
        e1own=vmem((NZ, TB, D), F32), e1send=vmem((NZ, TB, D), BF16), e1recv=vmem((NZ, TB, D), BF16),
        e2send=vmem((NZ - 1, TB, D), BF16), e2recv=vmem((NZ - 1, TB, D), BF16),
        e3send=vmem((NP, RB, D), BF16), e3recv=vmem((NP, RB, D), BF16),
        ld_m=dma((NS,)), ld_g=dma((NS,)), ld_x=dma((NS,)), ld_w=dma((3,)),
        a_send=dma((NS,)), a_recv=dma((NS,)), f_send=dma((NS,)), f_recv=dma((NS,)),
        d_send=dma((NP,)), d_recv=dma((NP,)), c_send=dma((NS,)), c_recv=dma((NS,)),
        t_send=dma, t_recv=dma, e1_s=dma, e1_r=dma,
        e2_s=dma((NZ - 1,)), e2_r=dma((NZ - 1,)), e3_s=dma((NP,)), e3_r=dma((NP,)),
    )
    hbm = pl.BlockSpec(memory_space=pl.ANY)
    local = pl.BlockSpec(memory_space=pltpu.VMEM)
    outs = pl.pallas_call(
        functools.partial(kernel, (NZ, NS, ROWS, F, D, T)),
        out_shape=(
            vmem(master.shape, F32),
            vmem(master.shape, F32),
            vmem((RB, D), BF16),
        ),
        in_specs=[hbm] * 6 + [local] * 2,
        out_specs=[local] * 3,
        scratch_shapes=list(scratch.values()),
        compiler_params=pltpu.CompilerParams(
            collective_id=0, has_side_effects=True, vmem_limit_bytes=48 * 1024 * 1024
        ),
        name="muon_rollout",
    )(master, momentum, gradient, up_weight, down_weight, tokens, routes.T, route_weight.T)
    return pl.pallas_call(
        hand_over,
        out_shape=tuple(jax.ShapeDtypeStruct(o.shape, o.dtype) for o in outs),
        in_specs=[hbm] * 3,
        out_specs=[hbm] * 3,
        scratch_shapes=[dma((3,))],
        compiler_params=pltpu.CompilerParams(vmem_limit_bytes=1024 * 1024),
        name="hand_over",
    )(*outs)


def solution(mesh):
    in_specs = (
        P("group", ("shard", "side"), None),
        P("group", ("shard", "side"), None),
        P("group", ("shard", "side"), None),
        P(("group", "shard"), "side", None),
        P(("group", "shard"), "side", None),
        P(),
        P(),
        P(),
    )
    out_specs = (
        P("group", ("shard", "side"), None),
        P("group", ("shard", "side"), None),
        P(("group", "shard", "side"), None),
    )
    return jax.shard_map(body, mesh=mesh, in_specs=in_specs, out_specs=out_specs, check_vma=False)
```

```python
import functools
import math

import jax
import jax.numpy as jnp
from jax import lax
from jax.experimental import pallas as pl
from jax.experimental.pallas import tpu as pltpu
from jax.sharding import PartitionSpec as P

NS_ITERS = 5
CAP = 128
CHUNKS = 2
MOMENTUM_BETA = 0.95
LEARN_RATE = 0.08
WEIGHT_DECAY = 0.1
NEWTON_A = 3.4445
NEWTON_B = -4.775
NEWTON_C = 2.0315
EPSILON = 1e-07
MESH = pl.DeviceIdType.MESH
F32 = jnp.float32
BF16 = jnp.bfloat16


def dot(a, b):
    return jnp.dot(a, b, preferred_element_type=F32)


def kernel(
    dims,
    master, momentum, gradient, up_hbm, down_hbm, tokens_hbm, routes, route_weight,
    mast, mom, comb,
    grad, sbuf, xbuf, mhalf, mbuf, obuf, osend,
    rf, rb, mb, tf, tb, qf, qb, tx, gx, gsend,
    upw, downw, tok, tok_o, tok_r, upv, hid, chosen,
    e1own, e1send, e1recv, e2send, e2recv, e2last, e2got, e3send, e3recv,
    ld_m, ld_g, ld_x, ld_w,
    a_send, a_recv, f_send, f_recv, d_send, d_recv, c_send, c_recv,
    t_send, t_recv, e1_s, e1_r, e2_s, e2_r, e3_s, e3_r,
):
    NZ, NS, ROWS, F, D, T = dims
    H = F // 2
    NP = 2 * NS
    TB = T // (2 * NZ)
    RB = TB // NP
    gi = lax.axis_index("group")
    z, k = gi // 2, gi % 2
    s = lax.axis_index("shard")
    a = lax.axis_index("side")
    same = a == k
    differ = a != k
    mine = s * 2 + a
    pgroup, pside = z * 2 + a, k
    sibling = {"group": z * 2 + 1 - k, "shard": s, "side": a}
    swap = {"group": z * 2 + 1 - k, "shard": s, "side": 1 - a}

    def remote(src, dst, send, recv, device):
        return pltpu.make_async_remote_copy(
            src_ref=src, dst_ref=dst, send_sem=send, recv_sem=recv,
            device_id=device, device_id_type=MESH,
        )

    def rows_of(r):
        return pl.ds(pl.multiple_of(r * ROWS, ROWS), ROWS)

    def load(j):
        pltpu.make_async_copy(momentum.at[j], mom.at[j], ld_m.at[j]).start()
        pltpu.make_async_copy(gradient.at[j], grad.at[j], ld_g.at[j]).start()

    NX = 4 if NS % 4 == 0 else NS
    NY = NS // NX
    cx, cy = lax.rem(s, NX), a * NY + s // NX

    def hop(t, sign):
        if NX != 4:
            return lax.rem(s + 2 * NS + sign * (1 + t), NS)
        u = t // NY
        dx = lax.rem(2 + 3 * u + 3 * (u * (u - 1) // 2), NX)
        dy = NY - 1 - lax.rem(t, NY)
        to_x = lax.rem(cx + NX + sign * dx, NX)
        to_y = lax.rem(s // NX + NY + sign * dy, NY)
        return to_y * NX + to_x

    def turn(t):
        return hop(t, 1)

    def origin(t):
        return hop(t, -1)

    def ring(n, i):
        return min(i, n - i)

    away_first = sorted(
        ((dx, dy) for dx in range(NX) for dy in range(2 * NY) if dx or dy),
        key=lambda o: -ring(NX, o[0]) - ring(2 * NY, o[1]),
    )

    def plane(offset):
        to_x, to_y = lax.rem(cx + offset[0], NX), lax.rem(cy + offset[1], 2 * NY)
        return lax.rem(to_y, NY) * NX + to_x, to_y // NY

    @pl.loop(0, NS)
    def _(t):
        load(turn(t))

    w_loads = [
        pltpu.make_async_copy(tokens_hbm, tok, ld_w.at[0]),
        pltpu.make_async_copy(up_hbm.at[0], upw, ld_w.at[1]),
        pltpu.make_async_copy(down_hbm.at[0], downw, ld_w.at[2]),
    ]

    barrier = pltpu.get_barrier_semaphore()

    def greet(device):
        pl.semaphore_signal(barrier, inc=1, device_id=device, device_id_type=MESH)

    @pl.loop(1, NP)
    def _(i):
        r = lax.rem(mine + i, NP)
        greet({"group": gi, "shard": r // 2, "side": lax.rem(r, 2)})

    @pl.loop(1, NZ)
    def _(i):
        greet({"group": lax.rem(z + i, NZ) * 2 + k, "shard": s, "side": a})

    greet(sibling)

    @pl.when(differ)
    def _():
        @pl.loop(0, NS)
        def _(j):
            greet({"group": pgroup, "shard": j, "side": pside})

    def a_copy(j):
        return remote(
            sbuf.at[j], xbuf.at[rows_of(mine)], a_send.at[j], a_recv.at[s],
            {"group": pgroup, "shard": j, "side": pside},
        )

    @pl.loop(0, NS)
    def _(t):
        j = turn(t)
        pltpu.make_async_copy(momentum.at[j], mom.at[j], ld_m.at[j]).wait()
        pltpu.make_async_copy(gradient.at[j], grad.at[j], ld_g.at[j]).wait()
        g = grad[j].astype(F32)
        m = MOMENTUM_BETA * mom[j] + g
        mom[j] = m
        sbuf[j] = (g + MOMENTUM_BETA * m).astype(BF16)

    @pl.when(differ)
    def _():
        pl.semaphore_wait(barrier, NP - 1 + NZ - 1 + 1 + NS)

    @pl.when(same)
    def _():
        pl.semaphore_wait(barrier, NP - 1 + NZ - 1 + 1)

    @pl.loop(0, NS)
    def _(t):
        j = turn(t)

        @pl.when(jnp.logical_not(jnp.logical_and(same, j == s)))
        def _():
            a_copy(j).start()

    @pl.when(same)
    def _():
        xbuf[rows_of(mine), :] = sbuf[s]

    for c in w_loads:
        c.start()

    @pl.loop(0, NS)
    def _(t):
        j = turn(t)
        pltpu.make_async_copy(master.at[j], mast.at[j], ld_x.at[j]).start()

    for c in w_loads:
        c.wait()
    token_row = lax.broadcasted_iota(jnp.int32, (T, T), 0)
    token_col = lax.broadcasted_iota(jnp.int32, (T, T), 1)
    upper = jnp.where(token_row <= token_col, 1.0, 0.0).astype(BF16)

    def slots(expert):
        hit = routes[...] == expert
        member = jnp.max(jnp.where(hit, 1.0, 0.0), axis=0, keepdims=True)
        rank = dot(jnp.broadcast_to(member, (16, T)).astype(BF16), upper)[:1]
        place = jnp.where(member > 0.5, rank - 1.0, -1.0)
        slot = lax.broadcasted_iota(jnp.int32, (CAP, T), 0).astype(F32)
        return jnp.where(slot == place, 1.0, 0.0), hit

    chosen_o, _ = slots((z * 2 + a) * NS + s)
    tok_o[...] = dot(chosen_o.astype(BF16), tok[...]).astype(BF16)
    chosen_r, hit_r = slots(gi * NS + s)
    tok_r[...] = dot(chosen_r.astype(BF16), tok[...]).astype(BF16)
    weight = jnp.sum(jnp.where(hit_r, route_weight[...], 0.0), axis=0, keepdims=True)
    weight = jnp.sum(chosen_r * weight, axis=1, keepdims=True)
    chosen[...] = chosen_r.astype(BF16)
    upv[...] = weight * lax.dot_general(
        tok_r[...], upw[...], (((1,), (1,)), ((), ())), preferred_element_type=F32
    )

    @pl.loop(0, NS)
    def _(t):
        j = turn(t)
        pltpu.make_async_copy(master.at[j], mast.at[j], ld_x.at[j]).wait()
        half = mast[j].astype(BF16)
        mhalf[j, 0] = half[:, :H]
        mhalf[j, 1] = half[:, H:]

    rf[...] = jnp.zeros_like(rf)
    tx[...] = jnp.zeros_like(tx)

    def f_copy(o, core):
        block = rows_of(o * 2 + core)
        return remote(xbuf.at[block], xbuf.at[block], f_send.at[o], f_recv.at[o], sibling)

    def gram(o):
        f_copy(o, 1 - k).wait_recv()
        pair = pl.ds(pl.multiple_of(o * 2 * ROWS, 2 * ROWS), 2 * ROWS)
        x = xbuf[pair, :]
        rf[...] += lax.dot_general(
            x, x, (((0,), (0,)), ((), ())), preferred_element_type=F32
        )
        tx[...] += dot(tok_o[:, pair], x)

    @pl.loop(0, NS)
    def _(t):
        o = origin(t)

        @pl.when(jnp.logical_not(jnp.logical_and(same, o == s)))
        def _():
            remote(
                sbuf.at[o], xbuf.at[rows_of(o * 2 + k)], a_send.at[o], a_recv.at[o],
                {"group": pgroup, "shard": o, "side": pside},
            ).wait_recv()

        f_copy(o, k).start()

        @pl.when(t > 0)
        def _():
            gram(origin(t - 1))

    def d_copy(j, h):
        return remote(
            mhalf.at[j, h], mbuf.at[rows_of(mine)], d_send.at[j * 2 + h], d_recv.at[mine],
            {"group": gi, "shard": j, "side": h},
        )

    for offset in away_first:
        d_copy(*plane(offset)).start()
    mbuf[rows_of(mine), :] = mhalf[s, a]

    gram(origin(NS - 1))

    B = 128
    eye = lax.broadcasted_iota(jnp.int32, (B, B), 0) == lax.broadcasted_iota(jnp.int32, (B, B), 1)
    blocks = [pl.ds(i * B, B) for i in range(F // B)]
    halves = [pl.ds(0, H), pl.ds(H, H)]

    def trace_of_rf():
        total = jnp.zeros((B, B), F32)
        for b in blocks:
            total = total + jnp.where(eye, rf[b, b], 0.0)
        return jnp.sum(total)

    def shift_rf(d):
        for b in blocks:
            v = rf[b, b] - jnp.where(eye, d, 0.0)
            rf[b, b] = v
            rb[b, b] = v.astype(BF16)

    scale = jnp.sqrt(trace_of_rf() + jnp.zeros((1, 1), F32))[0, 0]
    inverse = (1.0 / (jnp.zeros((1, 1), F32) + scale + EPSILON))[0, 0]
    for h in halves:
        v = rf[h, :] * inverse * inverse
        rf[h, :] = v
        rb[h, :] = v.astype(BF16)

    def recenter(d):
        move = trace_of_rf() * (1.0 / F)
        shift_rf(move)
        return d + move

    def form_mix(d):
        e1 = NEWTON_B + 2.0 * NEWTON_C * d
        for h in halves:
            mb[h, :] = (e1 * rf[h, :] + NEWTON_C * dot(rb[h, :], rb[...])).astype(BF16)
        return NEWTON_A + NEWTON_B * d + NEWTON_C * d * d

    def grow_q(lead, q):
        for h in halves:
            v = lead * qf[h, :] + q * mb[h, :].astype(F32) + dot(qb[h, :], mb[...])
            qf[h, :] = v
            qb[h, :] = v.astype(BF16)
        return q * lead

    def grow_g(lead, d):
        for h in halves:
            v = lead * rf[h, :] + d * mb[h, :].astype(F32) + dot(rb[h, :], mb[...])
            tf[h, :] = v
            tb[h, :] = v.astype(BF16)
        t = lead * d
        for h in halves:
            v = lead * tf[h, :] + t * mb[h, :].astype(F32) + dot(tb[h, :], mb[...])
            rf[h, :] = v
            rb[h, :] = v.astype(BF16)
        return lead * t

    d = recenter(jnp.float32(0.0))
    lead = form_mix(d)
    q = lead
    qf[...] = mb[...].astype(F32)
    qb[...] = mb[...]
    d = grow_g(lead, d)

    def iteration(_, carry):
        d, q = carry
        d = recenter(d)
        lead = form_mix(d)
        q = grow_q(lead, q)
        d = grow_g(lead, d)
        return d, q

    d, q = lax.fori_loop(1, NS_ITERS - 1, iteration, (d, q))
    d = recenter(d)
    lead = form_mix(d)
    q = grow_q(lead, q)

    cols = pl.ds(pl.multiple_of(k * H, H), H)
    part = inverse * (q * tx[:, cols] + dot(tx[...].astype(BF16), qb[:, cols]))
    t_copy = remote(gsend, gx, t_send, t_recv, swap)

    @pl.when(same)
    def _():
        gx[...] = part.astype(BF16)

    @pl.when(differ)
    def _():
        gsend[...] = part.astype(BF16)
        t_copy.start()

    def c_copy(o):
        return remote(
            osend.at[o], obuf.at[s], c_send.at[o], c_recv.at[s],
            {"group": pgroup, "shard": o, "side": pside},
        )

    BUNCH = min(4, NS)
    for first in range(0, NS, BUNCH):
        who = [turn(first + i) for i in range(BUNCH)]
        x = jnp.concatenate([xbuf[rows_of(o * 2 + k), :] for o in who], axis=0)
        y = (inverse * (q * x.astype(F32) + dot(x, qb[...]))).astype(BF16)
        for i, o in enumerate(who):
            osend[o] = y[i * ROWS:(i + 1) * ROWS]
            own = jnp.logical_and(same, o == s)

            @pl.when(own)
            def _():
                obuf[s] = osend[o]

            @pl.when(jnp.logical_not(own))
            def _():
                c_copy(o).start()

    @pl.loop(1, NP)
    def _(i):
        r = lax.rem(mine + i, NP)
        remote(
            mhalf.at[r // 2, lax.rem(r, 2)], mbuf.at[rows_of(r)], d_send.at[r], d_recv.at[r],
            {"group": gi, "shard": r // 2, "side": lax.rem(r, 2)},
        ).wait_recv()

    decay = 1.0 - LEARN_RATE * WEIGHT_DECAY
    step_scale = LEARN_RATE * 0.2 * math.sqrt(max(D, F))
    kept = decay * dot(tok_r[...], mbuf[...])

    @pl.when(differ)
    def _():
        t_copy.wait_recv()

    gate = kept - step_scale * gx[...].astype(F32)
    hidden = (gate * (1.0 / (1.0 + jnp.exp(-gate))) * upv[...]).astype(BF16)
    hid[...] = lax.dot_general(
        chosen[...], hidden, (((0,), (0,)), ((), ())), preferred_element_type=F32
    ).astype(BF16)

    def rows_for(core):
        parts = [pl.ds(pl.multiple_of((i * 2 + core) * TB, TB), TB) for i in range(NZ)]
        return jnp.concatenate([hid[p, :] for p in parts], axis=0)

    def e1_copy(c):
        return remote(e1send.at[c], e1recv.at[c], e1_s.at[c], e1_r.at[c], sibling)

    near = (z + 1 - 2 * lax.rem(z, 2), NZ - 1 - z)

    def e2_copy(c, i):
        peer = {"group": near[(c + i) % 2] * 2 + k, "shard": s, "side": a}
        if i == 0:
            return remote(e2send.at[c], e2recv.at[c], e2_s.at[c, 0], e2_r.at[c, 0], peer)
        return remote(e2last.at[c], e2got.at[c], e2_s.at[c, 1], e2_r.at[c, 1], peer)

    def e3_copy(c, j, h, slot):
        r = j * 2 + h
        return remote(
            e3send.at[c, r], e3recv.at[c, slot], e3_s.at[c, r], e3_r.at[c, slot],
            {"group": gi, "shard": j, "side": h},
        )

    WIDE = D // CHUNKS
    lanes = [slice(c * WIDE, (c + 1) * WIDE) for c in range(CHUNKS)]
    rows = rows_for(1 - k)
    for c in range(CHUNKS):
        e1send[c] = dot(rows, downw[:, lanes[c]]).astype(BF16)
        e1_copy(c).start()
    rows = rows_for(k)
    for c in range(CHUNKS):
        e1own[c] = dot(rows, downw[:, lanes[c]])

    def block(i):
        return pl.ds(pl.multiple_of(i * TB, TB), TB)

    def both(c, i):
        return e1own[c, block(i), :] + e1recv[c, block(i), :].astype(F32)

    for c in range(CHUNKS):
        first, second = near[c % 2], near[(c + 1) % 2]
        e1_copy(c).wait_recv()
        e2send[c, 0] = both(c, first).astype(BF16)
        e2send[c, 1] = both(c, NZ - 1 - first if c % 2 == 0 else first + 1 - 2 * lax.rem(first, 2)).astype(BF16)
        e2_copy(c, 0).start()
        e1own[c, block(z), :] = both(c, z)
        e1own[c, block(second), :] = both(c, second)
    for c in range(CHUNKS):
        second = near[(c + 1) % 2]
        e2_copy(c, 0).wait_recv()
        e2last[c] = (e1own[c, block(second), :] + e2recv[c, 1].astype(F32)).astype(BF16)
        e2_copy(c, 1).start()
    for c in range(CHUNKS):
        total = e1own[c, block(z), :] + e2recv[c, 0].astype(F32)
        e2_copy(c, 1).wait_recv()
        total = total + e2got[c].astype(F32)
        for r in range(NP):
            e3send[c, r] = total[r * RB:(r + 1) * RB].astype(BF16)
        for offset in away_first:
            e3_copy(c, *plane(offset), mine).start()
        e3recv[c, mine] = e3send[c, mine]

    @pl.loop(0, NS)
    def _(t):
        o = origin(t)

        @pl.when(jnp.logical_not(jnp.logical_and(same, o == s)))
        def _():
            remote(
                osend.at[o], obuf.at[o], c_send.at[o], c_recv.at[o],
                {"group": pgroup, "shard": o, "side": pside},
            ).wait_recv()

        mast[o] = decay * mast[o] - step_scale * obuf[o].astype(F32)

    for c in range(CHUNKS):
        @pl.loop(1, NP)
        def _(i):
            r = lax.rem(mine + i, NP)
            e3_copy(c, r // 2, lax.rem(r, 2), r).wait_recv()

        final = e3recv[c, 0].astype(F32)
        for r in range(1, NP):
            final = final + e3recv[c, r].astype(F32)
        comb[:, lanes[c]] = final.astype(BF16)

    @pl.loop(0, NS)
    def _(t):
        j = turn(t)

        @pl.when(jnp.logical_not(jnp.logical_and(same, j == s)))
        def _():
            a_copy(j).wait_send()
            c_copy(j).wait_send()

        f_copy(j, k).wait_send()

    @pl.loop(1, NP)
    def _(i):
        r = lax.rem(mine + i, NP)
        d_copy(r // 2, lax.rem(r, 2)).wait_send()
        for c in range(CHUNKS):
            e3_copy(c, r // 2, lax.rem(r, 2), mine).wait_send()

    for c in range(CHUNKS):
        e1_copy(c).wait_send()
        e2_copy(c, 0).wait_send()
        e2_copy(c, 1).wait_send()

    @pl.when(differ)
    def _():
        t_copy.wait_send()


def hand_over(master, momentum, combined, out_master, out_momentum, out_combined, sems):
    count = master.shape[0]
    copies = [pltpu.make_async_copy(combined, out_combined, sems.at[2 * count])]
    for j in range(count):
        copies.append(pltpu.make_async_copy(master.at[j], out_master.at[j], sems.at[j]))
        copies.append(pltpu.make_async_copy(momentum.at[j], out_momentum.at[j], sems.at[count + j]))
    for c in copies:
        c.start()
    for c in copies:
        c.wait()


def body(master, momentum, gradient, up_weight, down_weight, tokens, routes, route_weight):
    NS, ROWS, F = master.shape
    NZ = lax.axis_size("group") // 2
    T, D = tokens.shape
    H = F // 2
    NP = 2 * NS
    TB = T // (2 * NZ)
    RB = TB // NP
    WIDE = D // CHUNKS
    dma = pltpu.SemaphoreType.DMA
    vmem = pltpu.VMEM
    scratch = dict(
        grad=vmem((NS, ROWS, F), BF16),
        sbuf=vmem((NS, ROWS, F), BF16), xbuf=vmem((D, F), BF16), mhalf=vmem((NS, 2, ROWS, H), BF16),
        mbuf=vmem((D, H), BF16), obuf=vmem((NS, ROWS, F), BF16), osend=vmem((NS, ROWS, F), BF16),
        rf=vmem((F, F), F32), rb=vmem((F, F), BF16), mb=vmem((F, F), BF16), tf=vmem((F, F), F32),
        tb=vmem((F, F), BF16), qf=vmem((F, F), F32), qb=vmem((F, F), BF16), tx=vmem((CAP, F), F32),
        gx=vmem((CAP, H), BF16), gsend=vmem((CAP, H), BF16),
        upw=vmem((H, D), BF16), downw=vmem((H, D), BF16), tok=vmem((T, D), BF16),
        tok_o=vmem((CAP, D), BF16), tok_r=vmem((CAP, D), BF16), upv=vmem((CAP, H), F32),
        hid=vmem((T, H), BF16), chosen=vmem((CAP, T), BF16),
        e1own=vmem((CHUNKS, NZ * TB, WIDE), F32),
        e1send=vmem((CHUNKS, NZ * TB, WIDE), BF16), e1recv=vmem((CHUNKS, NZ * TB, WIDE), BF16),
        e2send=vmem((CHUNKS, 2, TB, WIDE), BF16), e2recv=vmem((CHUNKS, 2, TB, WIDE), BF16),
        e2last=vmem((CHUNKS, TB, WIDE), BF16), e2got=vmem((CHUNKS, TB, WIDE), BF16),
        e3send=vmem((CHUNKS, NP, RB, WIDE), BF16), e3recv=vmem((CHUNKS, NP, RB, WIDE), BF16),
        ld_m=dma((NS,)), ld_g=dma((NS,)), ld_x=dma((NS,)), ld_w=dma((3,)),
        a_send=dma((NS,)), a_recv=dma((NS,)), f_send=dma((NS,)), f_recv=dma((NS,)),
        d_send=dma((NP,)), d_recv=dma((NP,)), c_send=dma((NS,)), c_recv=dma((NS,)),
        t_send=dma, t_recv=dma, e1_s=dma((CHUNKS,)), e1_r=dma((CHUNKS,)),
        e2_s=dma((CHUNKS, 2)), e2_r=dma((CHUNKS, 2)),
        e3_s=dma((CHUNKS, NP)), e3_r=dma((CHUNKS, NP)),
    )
    hbm = pl.BlockSpec(memory_space=pl.ANY)
    local = pl.BlockSpec(memory_space=pltpu.VMEM)
    outs = pl.pallas_call(
        functools.partial(kernel, (NZ, NS, ROWS, F, D, T)),
        out_shape=(
            vmem(master.shape, F32),
            vmem(master.shape, F32),
            vmem((RB, D), BF16),
        ),
        in_specs=[hbm] * 6 + [local] * 2,
        out_specs=[local] * 3,
        scratch_shapes=list(scratch.values()),
        compiler_params=pltpu.CompilerParams(
            collective_id=0, has_side_effects=True, vmem_limit_bytes=48 * 1024 * 1024
        ),
        name="muon_rollout",
    )(master, momentum, gradient, up_weight, down_weight, tokens, routes.T, route_weight.T)
    return pl.pallas_call(
        hand_over,
        out_shape=tuple(jax.ShapeDtypeStruct(o.shape, o.dtype) for o in outs),
        in_specs=[hbm] * 3,
        out_specs=[hbm] * 3,
        scratch_shapes=[dma((2 * NS + 1,))],
        compiler_params=pltpu.CompilerParams(vmem_limit_bytes=1024 * 1024),
        name="hand_over",
    )(*outs)


def solution(mesh):
    in_specs = (
        P("group", ("shard", "side"), None),
        P("group", ("shard", "side"), None),
        P("group", ("shard", "side"), None),
        P(("group", "shard"), "side", None),
        P(("group", "shard"), "side", None),
        P(),
        P(),
        P(),
    )
    out_specs = (
        P("group", ("shard", "side"), None),
        P("group", ("shard", "side"), None),
        P(("group", "shard", "side"), None),
    )
    return jax.shard_map(body, mesh=mesh, in_specs=in_specs, out_specs=out_specs, check_vma=False)
```

```python
import functools
import math

import jax
import jax.numpy as jnp
from jax import lax
from jax.experimental import pallas as pl
from jax.experimental.pallas import tpu as pltpu
from jax.sharding import PartitionSpec as P

NS_ITERS = 5
CAP = 128
CHUNKS = 2
PIECES = 1
MOMENTUM_BETA = 0.95
LEARN_RATE = 0.08
WEIGHT_DECAY = 0.1
NEWTON_A = 3.4445
NEWTON_B = -4.775
NEWTON_C = 2.0315
EPSILON = 1e-07
MESH = pl.DeviceIdType.MESH
F32 = jnp.float32
BF16 = jnp.bfloat16


def dot(a, b):
    return jnp.dot(a, b, preferred_element_type=F32)


def kernel(
    dims,
    master, momentum, gradient, up_hbm, down_hbm, tokens_hbm, routes_hbm, route_weight_hbm,
    mast, mom, comb, obuf,
    grad, sbuf, xbuf, px_send, px_recv, py_send, py_recv, qx_send, qx_recv, qy_send, qy_recv, kept, places, tokc, osend,
    rf, rb, mb, tf, tb, qf, qb, tx, gx, gsend,
    upw, downw, tok, routes, route_weight, tok_o, tok_r, upv, hid, chosen,
    e1own, e1send, e1recv, e2send, e2recv, e2last, e2got, e3send, e3recv,
    ld_m, ld_g, ld_x, ld_w,
    a_send, a_recv, f_send, f_recv, px_s, px_r, py_s, py_r, qx_s, qx_r, qy_s, qy_r, c_send, c_recv,
    t_send, t_recv, e1_s, e1_r, e2_s, e2_r, e3_s, e3_r,
):
    NZ, NS, ROWS, F, D, T = dims
    H = F // 2
    NP = 2 * NS
    TB = T // (2 * NZ)
    RB = TB // NP
    gi = lax.axis_index("group")
    z, k = gi // 2, gi % 2
    s = lax.axis_index("shard")
    a = lax.axis_index("side")
    same = a == k
    differ = a != k
    mine = s * 2 + a
    pgroup, pside = z * 2 + a, k
    sibling = {"group": z * 2 + 1 - k, "shard": s, "side": a}
    swap = {"group": z * 2 + 1 - k, "shard": s, "side": 1 - a}

    def remote(src, dst, send, recv, device):
        return pltpu.make_async_remote_copy(
            src_ref=src, dst_ref=dst, send_sem=send, recv_sem=recv,
            device_id=device, device_id_type=MESH,
        )

    def rows_of(r):
        return pl.ds(pl.multiple_of(r * ROWS, ROWS), ROWS)

    def load(j):
        pltpu.make_async_copy(momentum.at[j], mom.at[j], ld_m.at[j]).start()
        pltpu.make_async_copy(gradient.at[j], grad.at[j], ld_g.at[j]).start()

    NX = 4 if NS % 4 == 0 else NS
    NY = NS // NX
    cx, cy = lax.rem(s, NX), a * NY + s // NX

    def hop(t, sign):
        if NX != 4:
            return lax.rem(s + 2 * NS + sign * (1 + t), NS)
        u = t // NY
        dx = lax.rem(2 + 3 * u + 3 * (u * (u - 1) // 2), NX)
        dy = NY - 1 - lax.rem(t, NY)
        to_x = lax.rem(cx + NX + sign * dx, NX)
        to_y = lax.rem(s // NX + NY + sign * dy, NY)
        return to_y * NX + to_x

    def turn(t):
        return hop(t, 1)

    def origin(t):
        return hop(t, -1)

    def ring(n, i):
        return min(i, n - i)

    away_first = sorted(
        ((dx, dy) for dx in range(NX) for dy in range(2 * NY) if dx or dy),
        key=lambda o: -ring(NX, o[0]) - ring(2 * NY, o[1]),
    )

    def plane(offset):
        to_x, to_y = lax.rem(cx + offset[0], NX), lax.rem(cy + offset[1], 2 * NY)
        return lax.rem(to_y, NY) * NX + to_x, to_y // NY

    @pl.loop(0, NS)
    def _(t):
        load(turn(t))

    w_loads = [
        pltpu.make_async_copy(tokens_hbm, tok, ld_w.at[0]),
        pltpu.make_async_copy(up_hbm.at[0], upw, ld_w.at[1]),
        pltpu.make_async_copy(down_hbm.at[0], downw, ld_w.at[2]),
        pltpu.make_async_copy(routes_hbm, routes, ld_w.at[3]),
        pltpu.make_async_copy(route_weight_hbm, route_weight, ld_w.at[4]),
    ]

    barrier = pltpu.get_barrier_semaphore()

    def greet(device):
        pl.semaphore_signal(barrier, inc=1, device_id=device, device_id_type=MESH)

    @pl.loop(1, NP)
    def _(i):
        r = lax.rem(mine + i, NP)
        greet({"group": gi, "shard": r // 2, "side": lax.rem(r, 2)})

    @pl.loop(1, NZ)
    def _(i):
        greet({"group": lax.rem(z + i, NZ) * 2 + k, "shard": s, "side": a})

    greet(sibling)

    @pl.when(differ)
    def _():
        @pl.loop(0, NS)
        def _(j):
            greet({"group": pgroup, "shard": j, "side": pside})

    PART = ROWS // PIECES

    def piece_of(r, u):
        return pl.ds(pl.multiple_of(r * ROWS + u * PART, PART), PART)

    def a_copy(j, u, row=mine, slot=s):
        return remote(
            sbuf.at[j, pl.ds(u * PART, PART)], xbuf.at[piece_of(row, u)],
            a_send.at[j, u], a_recv.at[slot, u],
            {"group": pgroup, "shard": j, "side": pside},
        )

    def blend(j):
        pltpu.make_async_copy(momentum.at[j], mom.at[j], ld_m.at[j]).wait()
        pltpu.make_async_copy(gradient.at[j], grad.at[j], ld_g.at[j]).wait()
        g = grad[j].astype(F32)
        m = MOMENTUM_BETA * mom[j] + g
        mom[j] = m
        sbuf[j] = (g + MOMENTUM_BETA * m).astype(BF16)

    blend(turn(0))

    @pl.when(differ)
    def _():
        pl.semaphore_wait(barrier, NP - 1 + NZ - 1 + 1 + NS)

    @pl.when(same)
    def _():
        pl.semaphore_wait(barrier, NP - 1 + NZ - 1 + 1)

    def partner(j):
        return jnp.logical_not(jnp.logical_and(same, j == s))

    @pl.loop(0, NS)
    def _(t):
        j = turn(t)

        @pl.when(t > 0)
        def _():
            blend(j)

        @pl.when(partner(j))
        def _():
            a_copy(j, 0).start()

    @pl.when(same)
    def _():
        xbuf[rows_of(mine), :] = sbuf[s]

    for c in w_loads:
        c.start()

    @pl.loop(0, NS)
    def _(t):
        j = turn(t)
        pltpu.make_async_copy(master.at[j], mast.at[j], ld_x.at[j]).start()

    for c in w_loads:
        c.wait()
    token_row = lax.broadcasted_iota(jnp.int32, (T, T), 0)
    token_col = lax.broadcasted_iota(jnp.int32, (T, T), 1)
    upper = jnp.where(token_row <= token_col, 1.0, 0.0).astype(BF16)

    def slots(expert):
        hit = routes[...] == expert
        member = jnp.max(jnp.where(hit, 1.0, 0.0), axis=0, keepdims=True)
        rank = dot(jnp.broadcast_to(member, (16, T)).astype(BF16), upper)[:1]
        place = jnp.where(member > 0.5, rank - 1.0, -1.0)
        slot = lax.broadcasted_iota(jnp.int32, (CAP, T), 0).astype(F32)
        return jnp.where(slot == place, 1.0, 0.0), hit

    chosen_o, _ = slots((z * 2 + a) * NS + s)
    tok_o[...] = dot(chosen_o.astype(BF16), tok[...]).astype(BF16)
    chosen_r, hit_r = slots(gi * NS + s)
    tok_r[...] = dot(chosen_r.astype(BF16), tok[...]).astype(BF16)
    weight = jnp.sum(jnp.where(hit_r, route_weight[...], 0.0), axis=0, keepdims=True)
    weight = jnp.sum(chosen_r * weight, axis=1, keepdims=True)
    chosen[...] = chosen_r.astype(BF16)
    upv[...] = weight * lax.dot_general(
        tok_r[...], upw[...], (((1,), (1,)), ((), ())), preferred_element_type=F32
    )

    HS = CAP // 2
    NYT = 2 * NY
    own_cols = pl.ds(pl.multiple_of(mine * ROWS, ROWS), ROWS)

    named = [
        jnp.max(jnp.where(routes[...] == gi * NS + j, 1.0, 0.0), axis=0, keepdims=True)
        for j in range(NS)
    ]
    named = jnp.concatenate(named + [jnp.zeros((16 - NS, T), F32)], axis=0)
    places[...] = jnp.where(named > 0.5, dot(named.astype(BF16), upper) - 1.0, -1.0)
    tokc[...] = tok[:, own_cols]

    @pl.loop(0, NS)
    def _(t):
        j = turn(t)
        pltpu.make_async_copy(master.at[j], mast.at[j], ld_x.at[j]).wait()
        slot = lax.broadcasted_iota(jnp.int32, (CAP, T), 0).astype(F32)
        taken = jnp.where(slot == places[pl.ds(j, 1), :], 1.0, 0.0).astype(BF16)
        picked = dot(taken, tokc[...]).astype(BF16)
        value = dot(picked, mast[j].astype(BF16)).astype(BF16)
        to_x, to_y = lax.rem(j, NX), j // NX
        px_send[to_x, to_y] = value[:HS, :H]
        px_send[to_x, to_y + NY] = value[:HS, H:]
        py_send[to_y, to_x] = value[HS:, :H]
        py_send[to_y + NY, to_x] = value[HS:, H:]

    def spot(offset):
        j, h = plane(offset)
        return {"group": gi, "shard": j, "side": h}

    def px_copy(i):
        src = px_send.at[lax.rem(cx + i, NX)]
        return remote(src, px_recv.at[i - 1], px_s.at[i - 1], px_r.at[i - 1], spot((i, 0)))

    def py_copy(i):
        src = py_send.at[lax.rem(cy + i, NYT)]
        return remote(src, py_recv.at[i - 1], py_s.at[i - 1], py_r.at[i - 1], spot((0, i)))

    def qx_copy(i):
        return remote(
            qx_send.at[i - 1], qx_recv.at[i - 1], qx_s.at[i - 1], qx_r.at[i - 1], spot((0, i))
        )

    def qy_copy(i):
        return remote(
            qy_send.at[i - 1], qy_recv.at[i - 1], qy_s.at[i - 1], qy_r.at[i - 1], spot((i, 0))
        )

    def second_stage():
        for i in range(1, NX):
            px_copy(i).wait_recv()
        for i in range(1, NYT):
            py_copy(i).wait_recv()

        def sum_x(y):
            v = px_send[cx, y].astype(F32)
            for i in range(NX - 1):
                v = v + px_recv[i, y].astype(F32)
            return v

        def sum_y(x):
            v = py_send[cy, x].astype(F32)
            for i in range(NYT - 1):
                v = v + py_recv[i, x].astype(F32)
            return v

        for i in range(1, NYT):
            qx_send[i - 1] = sum_x(lax.rem(cy + i, NYT)).astype(BF16)
            qx_copy(i).start()
        for i in range(1, NX):
            qy_send[i - 1] = sum_y(lax.rem(cx + i, NX)).astype(BF16)
            qy_copy(i).start()
        kept[:HS] = sum_x(cy)
        kept[HS:] = sum_y(cx)

    rf[...] = jnp.zeros_like(rf)
    tx[...] = jnp.zeros_like(tx)

    def f_copy(o, u, core):
        block = piece_of(o * 2 + core, u)
        return remote(xbuf.at[block], xbuf.at[block], f_send.at[o, u], f_recv.at[o, u], sibling)

    def arrive(o, u):
        @pl.when(jnp.logical_not(jnp.logical_and(same, o == s)))
        def _():
            a_copy(o, u, o * 2 + k, o).wait_recv()

        f_copy(o, u, k).start()

    def gram(o):
        for u in range(PIECES):
            f_copy(o, u, 1 - k).wait_recv()
        pair = pl.ds(pl.multiple_of(o * 2 * ROWS, 2 * ROWS), 2 * ROWS)
        x = xbuf[pair, :]
        rf[...] += lax.dot_general(
            x, x, (((0,), (0,)), ((), ())), preferred_element_type=F32
        )
        tx[...] += dot(tok_o[:, pair], x)

    for u in range(PIECES - 1):
        @pl.loop(0, NS)
        def _(t):
            arrive(origin(t), u)
            j = turn(t)

            @pl.when(partner(j))
            def _():
                a_copy(j, u).wait_send()
                a_copy(j, u + 1).start()

    @pl.loop(0, NS)
    def _(t):
        arrive(origin(t), PIECES - 1)

        @pl.when(t > 0)
        def _():
            gram(origin(t - 1))

    for i in range(1, NX):
        px_copy(i).start()
    for i in range(1, NYT):
        py_copy(i).start()
    gram(origin(NS - 1))

    B = 128
    eye = lax.broadcasted_iota(jnp.int32, (B, B), 0) == lax.broadcasted_iota(jnp.int32, (B, B), 1)
    blocks = [pl.ds(i * B, B) for i in range(F // B)]
    halves = [pl.ds(0, H), pl.ds(H, H)]

    def trace_of_rf():
        total = jnp.zeros((B, B), F32)
        for b in blocks:
            total = total + jnp.where(eye, rf[b, b], 0.0)
        return jnp.sum(total)

    def shift_rf(d):
        for b in blocks:
            v = rf[b, b] - jnp.where(eye, d, 0.0)
            rf[b, b] = v
            rb[b, b] = v.astype(BF16)

    scale = jnp.sqrt(trace_of_rf() + jnp.zeros((1, 1), F32))[0, 0]
    inverse = (1.0 / (jnp.zeros((1, 1), F32) + scale + EPSILON))[0, 0]
    for h in halves:
        v = rf[h, :] * inverse * inverse
        rf[h, :] = v
        rb[h, :] = v.astype(BF16)

    def recenter(d):
        move = trace_of_rf() * (1.0 / F)
        shift_rf(move)
        return d + move

    def form_mix(d):
        e1 = NEWTON_B + 2.0 * NEWTON_C * d
        for h in halves:
            mb[h, :] = (e1 * rf[h, :] + NEWTON_C * dot(rb[h, :], rb[...])).astype(BF16)
        return NEWTON_A + NEWTON_B * d + NEWTON_C * d * d

    def grow_q(lead, q):
        for h in halves:
            v = lead * qf[h, :] + q * mb[h, :].astype(F32) + dot(qb[h, :], mb[...])
            qf[h, :] = v
            qb[h, :] = v.astype(BF16)
        return q * lead

    def grow_g(lead, d):
        for h in halves:
            v = lead * rf[h, :] + d * mb[h, :].astype(F32) + dot(rb[h, :], mb[...])
            tf[h, :] = v
            tb[h, :] = v.astype(BF16)
        t = lead * d
        for h in halves:
            v = lead * tf[h, :] + t * mb[h, :].astype(F32) + dot(tb[h, :], mb[...])
            rf[h, :] = v
            rb[h, :] = v.astype(BF16)
        return lead * t

    d = recenter(jnp.float32(0.0))
    lead = form_mix(d)
    q = lead
    qf[...] = mb[...].astype(F32)
    qb[...] = mb[...]
    d = grow_g(lead, d)

    def iteration(_, carry):
        d, q = carry
        d = recenter(d)
        lead = form_mix(d)
        q = grow_q(lead, q)
        d = grow_g(lead, d)
        return d, q

    d, q = lax.fori_loop(1, NS_ITERS - 1, iteration, (d, q))
    second_stage()
    d = recenter(d)
    tx[...] = q * tx[...] + dot(tx[...].astype(BF16), qb[...])
    lead = form_mix(d)

    cols = pl.ds(pl.multiple_of(k * H, H), H)
    part = inverse * (lead * tx[:, cols] + dot(tx[...].astype(BF16), mb[:, cols]))
    t_copy = remote(gsend, gx, t_send, t_recv, swap)

    @pl.when(same)
    def _():
        gx[...] = part.astype(BF16)

    @pl.when(differ)
    def _():
        gsend[...] = part.astype(BF16)
        t_copy.start()

    q = grow_q(lead, q)

    def c_copy(o):
        return remote(
            osend.at[o], obuf.at[s], c_send.at[o], c_recv.at[s],
            {"group": pgroup, "shard": o, "side": pside},
        )

    BUNCH = min(4, NS)
    for first in range(0, NS, BUNCH):
        who = [turn(first + i) for i in range(BUNCH)]
        x = jnp.concatenate([xbuf[rows_of(o * 2 + k), :] for o in who], axis=0)
        y = (inverse * (q * x.astype(F32) + dot(x, qb[...]))).astype(BF16)
        for i, o in enumerate(who):
            osend[o] = y[i * ROWS:(i + 1) * ROWS]
            own = jnp.logical_and(same, o == s)

            @pl.when(own)
            def _():
                obuf[s] = osend[o]

            @pl.when(jnp.logical_not(own))
            def _():
                c_copy(o).start()

    for i in range(1, NYT):
        qx_copy(i).wait_recv()
        kept[:HS] += qx_recv[i - 1].astype(F32)
    for i in range(1, NX):
        qy_copy(i).wait_recv()
        kept[HS:] += qy_recv[i - 1].astype(F32)

    decay = 1.0 - LEARN_RATE * WEIGHT_DECAY
    step_scale = LEARN_RATE * 0.2 * math.sqrt(max(D, F))
    @pl.when(differ)
    def _():
        t_copy.wait_recv()

    gate = decay * kept[...] - step_scale * gx[...].astype(F32)
    hidden = (gate * (1.0 / (1.0 + jnp.exp(-gate))) * upv[...]).astype(BF16)
    hid[...] = lax.dot_general(
        chosen[...], hidden, (((0,), (0,)), ((), ())), preferred_element_type=F32
    ).astype(BF16)

    def rows_for(core):
        parts = [pl.ds(pl.multiple_of((i * 2 + core) * TB, TB), TB) for i in range(NZ)]
        return jnp.concatenate([hid[p, :] for p in parts], axis=0)

    def e1_copy(c):
        return remote(e1send.at[c], e1recv.at[c], e1_s.at[c], e1_r.at[c], sibling)

    near = (z + 1 - 2 * lax.rem(z, 2), NZ - 1 - z)

    def e2_copy(c, i):
        peer = {"group": near[(c + i) % 2] * 2 + k, "shard": s, "side": a}
        if i == 0:
            return remote(e2send.at[c], e2recv.at[c], e2_s.at[c, 0], e2_r.at[c, 0], peer)
        return remote(e2last.at[c], e2got.at[c], e2_s.at[c, 1], e2_r.at[c, 1], peer)

    def e3_copy(j, h, slot):
        r = j * 2 + h
        return remote(
            e3send.at[r], e3recv.at[slot], e3_s.at[r], e3_r.at[slot],
            {"group": gi, "shard": j, "side": h},
        )

    WIDE = D // CHUNKS
    lanes = [slice(c * WIDE, (c + 1) * WIDE) for c in range(CHUNKS)]
    rows = rows_for(1 - k)
    for c in range(CHUNKS):
        e1send[c] = dot(rows, downw[:, lanes[c]]).astype(BF16)
        e1_copy(c).start()
    rows = rows_for(k)
    for c in range(CHUNKS):
        e1own[c] = dot(rows, downw[:, lanes[c]])

    def block(i):
        return pl.ds(pl.multiple_of(i * TB, TB), TB)

    def both(c, i):
        return e1own[c, block(i), :] + e1recv[c, block(i), :].astype(F32)

    for c in range(CHUNKS):
        first, second = near[c % 2], near[(c + 1) % 2]
        e1_copy(c).wait_recv()
        e2send[c, 0] = both(c, first).astype(BF16)
        e2send[c, 1] = both(c, NZ - 1 - first if c % 2 == 0 else first + 1 - 2 * lax.rem(first, 2)).astype(BF16)
        e2_copy(c, 0).start()
        e1own[c, block(z), :] = both(c, z)
        e1own[c, block(second), :] = both(c, second)
    for c in range(CHUNKS):
        second = near[(c + 1) % 2]
        e2_copy(c, 0).wait_recv()
        e2last[c] = (e1own[c, block(second), :] + e2recv[c, 1].astype(F32)).astype(BF16)
        e2_copy(c, 1).start()
    for c in range(CHUNKS):
        total = e1own[c, block(z), :] + e2recv[c, 0].astype(F32)
        e2_copy(c, 1).wait_recv()
        total = total + e2got[c].astype(F32)
        for r in range(NP):
            e3send[r, :, lanes[c]] = total[r * RB:(r + 1) * RB].astype(BF16)
    for offset in away_first:
        e3_copy(*plane(offset), mine).start()
    e3recv[mine] = e3send[mine]

    @pl.loop(0, NS)
    def _(t):
        o = origin(t)

        @pl.when(jnp.logical_not(jnp.logical_and(same, o == s)))
        def _():
            remote(
                osend.at[o], obuf.at[o], c_send.at[o], c_recv.at[o],
                {"group": pgroup, "shard": o, "side": pside},
            ).wait_recv()


    @pl.loop(1, NP)
    def _(i):
        r = lax.rem(mine + i, NP)
        e3_copy(r // 2, lax.rem(r, 2), r).wait_recv()

    final = e3recv[0].astype(F32)
    for r in range(1, NP):
        final = final + e3recv[r].astype(F32)
    comb[...] = final.astype(BF16)

    @pl.loop(0, NS)
    def _(t):
        j = turn(t)

        @pl.when(jnp.logical_not(jnp.logical_and(same, j == s)))
        def _():
            a_copy(j, PIECES - 1).wait_send()
            c_copy(j).wait_send()

        for u in range(PIECES):
            f_copy(j, u, k).wait_send()

    @pl.loop(1, NP)
    def _(i):
        r = lax.rem(mine + i, NP)
        e3_copy(r // 2, lax.rem(r, 2), mine).wait_send()

    for i in range(1, NX):
        px_copy(i).wait_send()
        qy_copy(i).wait_send()
    for i in range(1, NYT):
        py_copy(i).wait_send()
        qx_copy(i).wait_send()
    for c in range(CHUNKS):
        e1_copy(c).wait_send()
        e2_copy(c, 0).wait_send()
        e2_copy(c, 1).wait_send()

    @pl.when(differ)
    def _():
        t_copy.wait_send()


def hand_over(step_scale, mast, mom, comb, rows, out_master, out_momentum, out_combined, new, sems):
    count = mast.shape[0]
    copies = [pltpu.make_async_copy(comb, out_combined, sems.at[2 * count])]
    for j in range(count):
        copies.append(pltpu.make_async_copy(mom.at[j], out_momentum.at[j], sems.at[count + j]))
    for c in copies:
        c.start()
    for j in range(count):
        new[j] = (1.0 - LEARN_RATE * WEIGHT_DECAY) * mast[j] - step_scale * rows[j].astype(F32)
        c = pltpu.make_async_copy(new.at[j], out_master.at[j], sems.at[j])
        c.start()
        copies.append(c)
    for c in copies:
        c.wait()


def body(master, momentum, gradient, up_weight, down_weight, tokens, routes, route_weight):
    NS, ROWS, F = master.shape
    NZ = lax.axis_size("group") // 2
    T, D = tokens.shape
    H = F // 2
    NP = 2 * NS
    TB = T // (2 * NZ)
    RB = TB // NP
    WIDE = D // CHUNKS
    NX = 4 if NS % 4 == 0 else NS
    NYT = 2 * NS // NX
    HS = CAP // 2
    MX = max(1, NX - 1)
    dma = pltpu.SemaphoreType.DMA
    vmem = pltpu.VMEM
    scratch = dict(
        grad=vmem((NS, ROWS, F), BF16),
        sbuf=vmem((NS, ROWS, F), BF16), xbuf=vmem((D, F), BF16),
        px_send=vmem((NX, NYT, HS, H), BF16), px_recv=vmem((MX, NYT, HS, H), BF16),
        py_send=vmem((NYT, NX, HS, H), BF16), py_recv=vmem((NYT - 1, NX, HS, H), BF16),
        qx_send=vmem((NYT - 1, HS, H), BF16), qx_recv=vmem((NYT - 1, HS, H), BF16),
        qy_send=vmem((MX, HS, H), BF16), qy_recv=vmem((MX, HS, H), BF16), kept=vmem((CAP, H), F32),
        places=vmem((16, T), F32), tokc=vmem((T, ROWS), BF16),
        osend=vmem((NS, ROWS, F), BF16),
        rf=vmem((F, F), F32), rb=vmem((F, F), BF16), mb=vmem((F, F), BF16), tf=vmem((F, F), F32),
        tb=vmem((F, F), BF16), qf=vmem((F, F), F32), qb=vmem((F, F), BF16), tx=vmem((CAP, F), F32),
        gx=vmem((CAP, H), BF16), gsend=vmem((CAP, H), BF16),
        upw=vmem((H, D), BF16), downw=vmem((H, D), BF16), tok=vmem((T, D), BF16),
        routes=vmem(routes.T.shape, jnp.int32), route_weight=vmem(routes.T.shape, F32),
        tok_o=vmem((CAP, D), BF16), tok_r=vmem((CAP, D), BF16), upv=vmem((CAP, H), F32),
        hid=vmem((T, H), BF16), chosen=vmem((CAP, T), BF16),
        e1own=vmem((CHUNKS, NZ * TB, WIDE), F32),
        e1send=vmem((CHUNKS, NZ * TB, WIDE), BF16), e1recv=vmem((CHUNKS, NZ * TB, WIDE), BF16),
        e2send=vmem((CHUNKS, 2, TB, WIDE), BF16), e2recv=vmem((CHUNKS, 2, TB, WIDE), BF16),
        e2last=vmem((CHUNKS, TB, WIDE), BF16), e2got=vmem((CHUNKS, TB, WIDE), BF16),
        e3send=vmem((NP, RB, D), BF16), e3recv=vmem((NP, RB, D), BF16),
        ld_m=dma((NS,)), ld_g=dma((NS,)), ld_x=dma((NS,)), ld_w=dma((5,)),
        a_send=dma((NS, PIECES)), a_recv=dma((NS, PIECES)),
        f_send=dma((NS, PIECES)), f_recv=dma((NS, PIECES)),
        px_s=dma((MX,)), px_r=dma((MX,)), py_s=dma((NYT - 1,)), py_r=dma((NYT - 1,)),
        qx_s=dma((NYT - 1,)), qx_r=dma((NYT - 1,)), qy_s=dma((MX,)), qy_r=dma((MX,)),
        c_send=dma((NS,)), c_recv=dma((NS,)),
        t_send=dma, t_recv=dma, e1_s=dma((CHUNKS,)), e1_r=dma((CHUNKS,)),
        e2_s=dma((CHUNKS, 2)), e2_r=dma((CHUNKS, 2)),
        e3_s=dma((NP,)), e3_r=dma((NP,)),
    )
    hbm = pl.BlockSpec(memory_space=pl.ANY)
    local = pl.BlockSpec(memory_space=pltpu.VMEM)
    outs = pl.pallas_call(
        functools.partial(kernel, (NZ, NS, ROWS, F, D, T)),
        out_shape=(
            vmem(master.shape, F32),
            vmem(master.shape, F32),
            vmem((RB, D), BF16),
            vmem(master.shape, BF16),
        ),
        in_specs=[hbm] * 8,
        out_specs=[local] * 4,
        scratch_shapes=list(scratch.values()),
        compiler_params=pltpu.CompilerParams(
            collective_id=0, has_side_effects=True, vmem_limit_bytes=48 * 1024 * 1024
        ),
        name="muon_rollout",
    )(master, momentum, gradient, up_weight, down_weight, tokens, routes.T, route_weight.T)
    return pl.pallas_call(
        functools.partial(hand_over, LEARN_RATE * 0.2 * math.sqrt(max(D, F))),
        out_shape=tuple(jax.ShapeDtypeStruct(o.shape, o.dtype) for o in outs[:3]),
        in_specs=[local] * 4,
        out_specs=[hbm] * 3,
        scratch_shapes=[vmem(master.shape, F32), dma((2 * NS + 1,))],
        compiler_params=pltpu.CompilerParams(vmem_limit_bytes=8 * 1024 * 1024),
        name="hand_over",
    )(*outs)


def solution(mesh):
    in_specs = (
        P("group", ("shard", "side"), None),
        P("group", ("shard", "side"), None),
        P("group", ("shard", "side"), None),
        P(("group", "shard"), "side", None),
        P(("group", "shard"), "side", None),
        P(),
        P(),
        P(),
    )
    out_specs = (
        P("group", ("shard", "side"), None),
        P("group", ("shard", "side"), None),
        P(("group", "shard", "side"), None),
    )
    return jax.shard_map(body, mesh=mesh, in_specs=in_specs, out_specs=out_specs, check_vma=False)
```
